1024 devices in a mesh: row: 32 (over z, core), col: 32 (over x, y).
Axes of the slice: x: 4, y: 8, z: 16, core: 2. Of those that a mesh axis runs over, the one named last changes fastest.
Arguments:
- matrix: float32 [20480, 20480], P('row', 'col'), may hold values from -16 to 16, as said below
Outputs:
- reduced: float32 [20480, 20480], P('row', 'col')
The draws below stay inside these ranges and needn't reach their ends.
Inputs may be any that keep to these rules, and one draw needn't show every extreme that they name: matrix is exactly symmetric.
All inputs are finite; a program needn't handle non-finite values.
Results may differ from the reference program's by a relative error of at most 0.0015.
Values may be sent and summed in bfloat16 or wider, within the bound.
A program may use at most 32 MiB of HBM per device.

```python
import math
import jax
import jax.numpy as jnp
from jax import lax

PW = 64
ORDER = 20480
N_ROW = 32


def draw_matrix(key, part):
    keys = jax.random.split(key, 2)
    noise = jnp.clip(jax.random.normal(keys[0], (ORDER, ORDER), jnp.float32), -4.0, 4.0)
    scales = jnp.exp(jax.random.uniform(keys[1], (ORDER,), jnp.float32, math.log(0.4), math.log(1.6)))
    symmetric = (noise + noise.T) * 0.70710678
    total = scales[:, None] * scales[None, :] * symmetric
    return total


def setup_inputs(seed: int = 0) -> dict:
    key_list = jax.random.split(jax.random.key(seed), 2)
    return {
        "matrix": draw_matrix(jax.random.fold_in(key_list[1], 71), 0),
    }


HIGHEST = lax.Precision.HIGHEST

def reference(matrix):
    matrix_order = matrix.shape[0]
    positions = jnp.arange(matrix_order, dtype=jnp.int32)
    left_part = jnp.where((positions >= PW)[:, None], matrix[:, :PW], jnp.float32(0.0))
    gram_matrix = jnp.dot(left_part.T.astype(jnp.float32), left_part.astype(jnp.float32), precision=HIGHEST, preferred_element_type=jnp.float32)
    upper_factor = jnp.linalg.cholesky(gram_matrix).T
    shifted_top = matrix[PW:2 * PW, :PW] + upper_factor
    coupling = jnp.dot(shifted_top.T.astype(jnp.float32), upper_factor.astype(jnp.float32), precision=HIGHEST, preferred_element_type=jnp.float32)
    core_inverse = jnp.linalg.inv(coupling)
    offsets = positions - PW
    picker = (offsets[:, None] == jnp.arange(PW, dtype=jnp.int32)[None, :]).astype(jnp.float32)
    basis = (left_part + jnp.dot(picker.astype(jnp.float32), upper_factor.astype(jnp.float32), precision=HIGHEST, preferred_element_type=jnp.float32)).astype(jnp.bfloat16)
    matrix_half = matrix.astype(jnp.bfloat16)
    images = jnp.dot(matrix_half.astype(jnp.float32), basis.astype(jnp.float32), preferred_element_type=jnp.float32)
    basis_wide = basis.astype(jnp.float32)
    projection = jnp.dot(basis_wide.T.astype(jnp.float32), images.astype(jnp.float32), precision=HIGHEST, preferred_element_type=jnp.float32)
    middle = jnp.dot(jnp.dot(core_inverse.T.astype(jnp.float32), projection.astype(jnp.float32), precision=HIGHEST, preferred_element_type=jnp.float32).astype(jnp.float32), core_inverse.astype(jnp.float32), precision=HIGHEST, preferred_element_type=jnp.float32)
    update = (jnp.dot(images.astype(jnp.float32), core_inverse.astype(jnp.float32), precision=HIGHEST, preferred_element_type=jnp.float32) - 0.5 * jnp.dot(basis_wide.astype(jnp.float32), middle.astype(jnp.float32), precision=HIGHEST, preferred_element_type=jnp.float32)).astype(jnp.bfloat16)
    left_side = jnp.concatenate([basis, update], axis=1)
    right_side = jnp.concatenate([update, basis], axis=1)
    block_rows = matrix_order // N_ROW
    matrix_blocks = matrix.reshape(N_ROW, block_rows, matrix_order)
    left_blocks = left_side.reshape(N_ROW, block_rows, 2 * PW)

    def update_block(pair):
        product = lax.dot_general(pair[1].astype(jnp.float32), right_side.astype(jnp.float32), (((1,), (1,)), ((), ())), preferred_element_type=jnp.float32)
        return pair[0] - product
    result = lax.map(update_block, (matrix_blocks, left_blocks))
    return result.reshape(matrix_order, matrix_order)
```

```python
import functools

import jax
import jax.numpy as jnp
from jax import lax
from jax.experimental import pallas as pl
from jax.experimental.pallas import tpu as pltpu
from jax.sharding import PartitionSpec as P

PW = 64
HIGHEST = lax.Precision.HIGHEST
MESH = pl.DeviceIdType.MESH
F32 = jnp.float32
BF16 = jnp.bfloat16


def dot(first, second, dims, precision=None):
    return lax.dot_general(
        first, second, (dims, ((), ())), precision=precision, preferred_element_type=F32
    )


def far_first(count):
    return sorted(range(1, count), key=lambda d: -min(d, count - d))


def exchange(shape, a_ref, rowp_ref, colp_ref, gpart_ref,
             li_out, lj_out, zi_out, zj_out, g_out, k_out,
             li, lj, zp, zs, zr, zx, zi, zj, gs, gr, gx, g, kp, ks, kz, kc, kf, kk,
             send_z, recv_z, send_y, recv_y, send_x, recv_x, send_k, recv_k,
             send_b, recv_b, send_c, recv_c):
    nz, nx, ny = shape
    row, col = lax.axis_index("row"), lax.axis_index("col")
    z, c = row // 2, row % 2
    x, y = col // ny, col % ny
    partner = (z * 2 + 1 - c, col)

    def at_z(d):
        return (lax.rem(z + d, nz) * 2 + c, col)

    def at_y(d):
        return (row, x * ny + lax.rem(y + d, ny))

    def at_x(d):
        return (row, lax.rem(x + d, nx) * ny + y)

    def copy(src, dst, send, recv, where):
        return pltpu.make_async_remote_copy(
            src_ref=src, dst_ref=dst, send_sem=send, recv_sem=recv,
            device_id=where, device_id_type=MESH,
        )

    def got(ref, sem):
        copy(ref, ref, sem, sem, partner).wait_recv()

    def sent(ref, sem):
        copy(ref, ref, sem, sem, partner).wait_send()

    barrier = pltpu.get_barrier_semaphore()
    peers = [at_z(d) for d in range(1, nz)] + [at_y(d) for d in range(1, ny)]
    peers += [at_x(d) for d in range(1, nx)] + [partner]
    for peer in peers:
        pl.semaphore_signal(barrier, inc=1, device_id=peer, device_id_type=MESH)
    pl.semaphore_wait(barrier, len(peers))

    @pl.when(row == 0)
    def _():
        for d in far_first(nz):
            copy(colp_ref.at[0], lj.at[0], send_z.at[0, d], recv_b.at[0], at_z(d)).start()
        copy(colp_ref.at[0], lj.at[0], send_c.at[0], recv_b.at[0], partner).start()

    @pl.when(col == 0)
    def _():
        for d in far_first(ny):
            copy(rowp_ref.at[d], li.at[d], send_y.at[0, d], recv_b.at[3], at_y(d)).start()
        for d in range(1, nx):
            copy(rowp_ref.at[0], li.at[0], send_x.at[0, d], recv_x.at[0, 0], at_x(d)).start()
        li[0] = rowp_ref[0]

    @pl.when(row == 0)
    def _():
        for d in far_first(ny):
            there = lax.rem(y + d, ny)
            copy(gpart_ref.at[there], gs.at[d], send_y.at[1, d], recv_y.at[1, d], at_y(d)).start()
        lj[...] = colp_ref[...]

    @pl.when((x == 0) & (y != 0))
    def _():
        got(li.at[y], recv_b.at[3])
        for d in range(1, nx):
            copy(li.at[y], li.at[y], send_x.at[0, d], recv_x.at[0, 0], at_x(d)).start()

    @pl.when(x != 0)
    def _():
        got(li.at[y], recv_x.at[0, 0])

    @pl.when(col == 0)
    def _():
        for d in far_first(ny):
            copy(rowp_ref.at[0], li.at[0], send_y.at[2, d], recv_y.at[2, d], at_y(d)).start()

    @pl.when(col != 0)
    def _():
        for d in far_first(ny):
            copy(li.at[y], li.at[y], send_y.at[2, d], recv_y.at[2, d], at_y(d)).start()

    @pl.when((row != 0) & (c == 0))
    def _():
        got(lj.at[0], recv_b.at[0])
        copy(lj.at[0], lj.at[0], send_c.at[0], recv_b.at[0], partner).start()

    @pl.when(c == 1)
    def _():
        got(lj.at[0], recv_b.at[0])

    part = dot(lj[0], a_ref[...].astype(BF16), ((1,), (1,)))
    zp[...] = part.reshape(zp.shape)
    for d in far_first(ny):
        there = lax.rem(y + d, ny)
        copy(zp.at[there], zs.at[d], send_y.at[3, d], recv_y.at[3, d], at_y(d)).start()

    @pl.when(row == 0)
    def _():
        total = gpart_ref[y]
        for d in range(1, ny):
            got(gs.at[d], recv_y.at[1, d])
            total += gs[d]
        gr[...] = total
        for d in range(1, nx):
            copy(gr, gx.at[d], send_x.at[1, d], recv_x.at[1, d], at_x(d)).start()
        for d in range(1, nx):
            got(gx.at[d], recv_x.at[1, d])
            total += gx[d]
        g[y] = total
        for d in far_first(ny):
            copy(g.at[y], g.at[y], send_y.at[4, d], recv_y.at[4, d], at_y(d)).start()

    total = zp[y]
    for d in range(1, ny):
        got(zs.at[d], recv_y.at[3, d])
        total += zs[d]
    zr[...] = total
    for d in range(1, nx):
        copy(zr, zx.at[d], send_x.at[2, d], recv_x.at[2, d], at_x(d)).start()
    for d in range(1, nx):
        got(zx.at[d], recv_x.at[2, d])
        total += zx[d]
    zi[y] = total
    for d in far_first(ny):
        copy(zi.at[y], zi.at[y], send_y.at[5, d], recv_y.at[5, d], at_y(d)).start()

    for d in range(1, ny):
        from_y = lax.rem(y + ny - d, ny)
        got(li.at[from_y], recv_y.at[2, d])
    panel = li[...].reshape(li.shape[0] * li.shape[1], li.shape[2]).astype(F32)
    mine = dot(total, panel, ((1,), (1,)), HIGHEST)
    kp[...] = mine
    for d in far_first(nz):
        copy(kp, ks.at[d], send_k.at[d], recv_k.at[d], at_z(d)).start()

    for d in range(1, ny):
        from_y = lax.rem(y + ny - d, ny)
        got(zi.at[from_y], recv_y.at[5, d])

    @pl.when(row == col)
    def _():
        for d in far_first(nz):
            copy(zi, zj, send_z.at[1, d], recv_b.at[1], at_z(d)).start()
        copy(zi, zj, send_c.at[1], recv_b.at[1], partner).start()

    @pl.when(row == 0)
    def _():
        for d in range(1, ny):
            from_y = lax.rem(y + ny - d, ny)
            got(g.at[from_y], recv_y.at[4, d])
        for d in far_first(nz):
            copy(g, g, send_z.at[2, d], recv_b.at[2], at_z(d)).start()
        copy(g, g, send_c.at[2], recv_b.at[2], partner).start()
        for d in far_first(nz):
            copy(colp_ref.at[1], lj.at[1], send_z.at[3, d], recv_b.at[4], at_z(d)).start()
        copy(colp_ref.at[1], lj.at[1], send_c.at[3], recv_b.at[4], partner).start()

    for d in range(1, nz):
        got(ks.at[d], recv_k.at[d])
        mine += ks[d]
    kz[...] = mine
    copy(kz, kc, send_c.at[4], recv_c.at[0], partner).start()
    got(kc, recv_c.at[0])
    kf[...] = mine + kc[...]
    for d in far_first(ny):
        copy(kf, kk.at[y], send_y.at[6, d], recv_y.at[6, d], at_y(d)).start()
    kk[y] = mine + kc[...]

    @pl.when((row != 0) & (c == 0))
    def _():
        got(g, recv_b.at[2])
        copy(g, g, send_c.at[2], recv_b.at[2], partner).start()
        got(lj.at[1], recv_b.at[4])
        copy(lj.at[1], lj.at[1], send_c.at[3], recv_b.at[4], partner).start()

    @pl.when((row != col) & (c == col % 2))
    def _():
        got(zj, recv_b.at[1])
        copy(zj, zj, send_c.at[1], recv_b.at[1], partner).start()

    @pl.when(c == 1)
    def _():
        got(g, recv_b.at[2])
        got(lj.at[1], recv_b.at[4])

    @pl.when(c != col % 2)
    def _():
        got(zj, recv_b.at[1])

    for d in range(1, ny):
        from_y = lax.rem(y + ny - d, ny)
        got(kk.at[from_y], recv_y.at[6, d])

    li_out[...] = li[...]
    lj_out[...] = lj[...]
    zi_out[...] = zi[...]
    g_out[...] = g[...]
    k_out[...] = kk[...]

    @pl.when(row == col)
    def _():
        zj_out[...] = zi[...]

    @pl.when(row != col)
    def _():
        zj_out[...] = zj[...]

    for d in range(1, ny):
        sent(li.at[0], send_y.at[2, d])
        sent(zr, send_y.at[3, d])
        sent(zr, send_y.at[5, d])
        sent(kp, send_y.at[6, d])
    for d in range(1, nx):
        sent(zr, send_x.at[2, d])
    for d in range(1, nz):
        sent(kp, send_k.at[d])
    sent(kp, send_c.at[4])

    @pl.when(x == 0)
    def _():
        for d in range(1, nx):
            sent(li.at[0], send_x.at[0, d])

    @pl.when(col == 0)
    def _():
        for d in range(1, ny):
            sent(li.at[0], send_y.at[0, d])

    @pl.when(row == 0)
    def _():
        for d in range(1, ny):
            sent(gr, send_y.at[1, d])
            sent(gr, send_y.at[4, d])
        for d in range(1, nx):
            sent(gr, send_x.at[1, d])
        for d in range(1, nz):
            sent(lj.at[0], send_z.at[0, d])
            sent(g, send_z.at[2, d])
            sent(lj.at[1], send_z.at[3, d])

    @pl.when(c == 0)
    def _():
        sent(lj.at[0], send_c.at[0])
        sent(g, send_c.at[2])
        sent(lj.at[1], send_c.at[3])

    @pl.when(c == col % 2)
    def _():
        sent(zi, send_c.at[1])

    @pl.when(row == col)
    def _():
        for d in range(1, nz):
            sent(zi, send_z.at[1, d])


def finish(a_ref, li_ref, lj_ref, zi_ref, zj_ref, g_ref, k_ref, out_ref):
    row, col = lax.axis_index("row"), lax.axis_index("col")
    size = a_ref.shape[1]
    rows = lax.broadcasted_iota(jnp.int32, (PW, PW), 0)
    lanes = lax.broadcasted_iota(jnp.int32, (PW, PW), 1)
    gram, cross = g_ref[0:PW, 0:PW], g_ref[0:PW, PW : 2 * PW]
    top, top_right = g_ref[PW : 2 * PW, 0:PW], g_ref[PW : 2 * PW, PW : 2 * PW]

    work = gram
    for i in range(PW):
        scale = work[:, i : i + 1] / work[i : i + 1, i : i + 1]
        work = work - jnp.where(rows[:, :1] > i, scale, 0.0) * work[i : i + 1, :]
    diagonal = jnp.sum(jnp.where(rows == lanes, work, 0.0), axis=1, keepdims=True)
    upper = jnp.where(lanes >= rows, work, 0.0) / jnp.sqrt(diagonal)

    shifted = top + upper
    coupling = dot(shifted, upper, ((0,), (0,)), HIGHEST)
    unit = jnp.where(rows == lanes, 1.0, 0.0).astype(F32)
    work = jnp.concatenate([coupling, unit], axis=1)
    tall = lax.broadcasted_iota(jnp.int32, (PW, 1), 0)
    for i in range(PW):
        pivot = work[i : i + 1, :] / work[i : i + 1, i : i + 1]
        work = jnp.where(tall == i, pivot, work - work[:, i : i + 1] * pivot)
    core = work[:, PW : 2 * PW]

    corner = shifted.astype(BF16)
    change = corner.astype(F32) - top.astype(BF16).astype(F32)
    side = dot(cross, change, ((1,), (0,)), HIGHEST)
    projection = k_ref[:, 0:PW] + side + dot(change, cross, ((0,), (1,)), HIGHEST)
    inner = dot(top_right, change, ((1,), (0,)), HIGHEST)
    projection = projection + dot(change, inner, ((0,), (0,)), HIGHEST)
    middle = dot(core, projection, ((0,), (0,)), HIGHEST)
    middle = dot(middle, core, ((1,), (0,)), HIGHEST)
    corner_t = corner.astype(F32).T

    def pair(left, right, images, first):
        ahead = left[:, 0 : 2 * PW]
        spread = jnp.concatenate([jnp.zeros((PW, PW), F32), corner_t], axis=1)
        wide = lax.broadcasted_iota(jnp.int32, (PW, 2 * PW), 1)
        placed = jnp.where((wide >= PW) & first, spread, ahead.astype(F32))
        basis = jnp.concatenate([placed.astype(BF16), left[:, 2 * PW :]], axis=1)
        full = images + dot(change, right.astype(F32), ((0,), (0,)), HIGHEST)
        update = dot(core, full, ((0,), (0,)), HIGHEST)
        update = update - 0.5 * dot(middle, basis.astype(F32), ((0,), (0,)), HIGHEST)
        return basis, update.astype(BF16)

    basis_i, update_i = pair(li_ref[0], li_ref[1], zi_ref[...], row == 0)
    basis_j, update_j = pair(lj_ref[0], lj_ref[1], zj_ref[...], col == 0)
    left = jnp.concatenate([basis_i, update_i], axis=0)
    right = jnp.concatenate([update_j, basis_j], axis=0)
    for i in range(0, size, 128):
        out_ref[i : i + 128, :] = a_ref[i : i + 128, :] - dot(
            left[:, i : i + 128], right, ((0,), (0,))
        )


def on_device(shape, matrix):
    nz, nx, ny = shape
    size = matrix.shape[0]
    row, col = lax.axis_index("row"), lax.axis_index("col")
    places = jnp.arange(size, dtype=jnp.int32)
    bands = jnp.arange(2 * PW, dtype=jnp.int32)[:, None]
    row_panel = jnp.where(
        (row == 0) & (places < PW)[None, :] & (bands < PW), 0.0, matrix[:, : 2 * PW].T
    )
    col_panel = jnp.where(
        (col == 0) & (places < PW)[None, :] & (bands < PW), 0.0, matrix[: 2 * PW, :]
    )
    left = col_panel[:PW]
    gram = dot(left, left, ((1,), (1,)), HIGHEST)
    half = col_panel.astype(BF16)
    cross = dot(half[:PW], half[PW:], ((1,), (1,)))
    top = jnp.where(col == 0, matrix[PW : 2 * PW, : 2 * PW], 0.0)
    top = jnp.concatenate([top[:, :PW], top[:, PW:].astype(BF16).astype(F32)], axis=1)
    gram_part = jnp.concatenate([jnp.concatenate([gram, cross], axis=1), top], axis=0)

    tall, low = 2 * PW // ny, PW // ny
    vmem = pl.BlockSpec(memory_space=pltpu.VMEM)
    dma = pltpu.SemaphoreType.DMA
    out_shape = (
        jax.ShapeDtypeStruct((ny, tall, size), BF16),
        jax.ShapeDtypeStruct((2, PW, size), BF16),
        jax.ShapeDtypeStruct((ny, low, size), F32),
        jax.ShapeDtypeStruct((ny, low, size), F32),
        jax.ShapeDtypeStruct((ny, tall, 2 * PW), F32),
        jax.ShapeDtypeStruct((ny, low, 2 * PW), F32),
    )
    scratch = [
        pltpu.VMEM((ny, tall, size), BF16),
        pltpu.VMEM((2, PW, size), BF16),
        pltpu.VMEM((ny, low, size), F32),
        pltpu.VMEM((ny, low, size), F32),
        pltpu.VMEM((low, size), F32),
        pltpu.VMEM((nx, low, size), F32),
        pltpu.VMEM((ny, low, size), F32),
        pltpu.VMEM((ny, low, size), F32),
        pltpu.VMEM((ny, tall, 2 * PW), F32),
        pltpu.VMEM((tall, 2 * PW), F32),
        pltpu.VMEM((nx, tall, 2 * PW), F32),
        pltpu.VMEM((ny, tall, 2 * PW), F32),
        pltpu.VMEM((low, 2 * PW), F32),
        pltpu.VMEM((nz, low, 2 * PW), F32),
        pltpu.VMEM((low, 2 * PW), F32),
        pltpu.VMEM((low, 2 * PW), F32),
        pltpu.VMEM((low, 2 * PW), F32),
        pltpu.VMEM((ny, low, 2 * PW), F32),
        dma((4, nz)), dma((1,)), dma((7, ny)), dma((7, ny)), dma((3, nx)), dma((3, nx)),
        dma((nz,)), dma((nz,)), dma((1,)), dma((5,)), dma((5,)), dma((1,)),
    ]
    li, lj, zi, zj, g, k = pl.pallas_call(
        functools.partial(exchange, shape),
        out_shape=out_shape,
        in_specs=[vmem] * 4,
        out_specs=(vmem,) * 6,
        scratch_shapes=scratch,
        compiler_params=pltpu.CompilerParams(collective_id=0, has_side_effects=True),
        name="exchange",
    )(
        matrix,
        row_panel.astype(BF16).reshape(ny, tall, size),
        half.reshape(2, PW, size),
        gram_part.reshape(ny, tall, 2 * PW),
    )
    return pl.pallas_call(
        finish,
        out_shape=jax.ShapeDtypeStruct(matrix.shape, F32),
        in_specs=[vmem] * 7,
        out_specs=vmem,
        name="finish",
    )(
        matrix,
        li.reshape(2, PW, size),
        lj,
        zi.reshape(PW, size),
        zj.reshape(PW, size),
        g.reshape(2 * PW, 2 * PW),
        k.reshape(PW, 2 * PW),
    )


def grid_of(mesh):
    rows, cols = mesh.shape["row"], mesh.shape["col"]
    return {(32, 32): (16, 4, 8), (4, 4): (2, 2, 2)}[(rows, cols)]


def solution(mesh):
    return jax.shard_map(
        functools.partial(on_device, grid_of(mesh)),
        mesh=mesh,
        in_specs=(P("row", "col"),),
        out_specs=P("row", "col"),
        check_vma=False,
    )
```

```python
import functools

import jax
import jax.numpy as jnp
from jax import lax
from jax.experimental import pallas as pl
from jax.experimental.pallas import tpu as pltpu
from jax.sharding import PartitionSpec as P

PW = 64
HIGHEST = lax.Precision.HIGHEST
MESH = pl.DeviceIdType.MESH
F32 = jnp.float32
BF16 = jnp.bfloat16


def dot(first, second, dims, precision=None):
    return lax.dot_general(
        first, second, (dims, ((), ())), precision=precision, preferred_element_type=F32
    )


def far_first(count):
    return sorted(range(1, count), key=lambda d: -min(d, count - d))


def eliminate(gram):
    rows = lax.broadcasted_iota(jnp.int32, (PW, PW), 0)
    lanes = lax.broadcasted_iota(jnp.int32, (PW, PW), 1)
    work = gram
    for i in range(PW):
        scale = work[:, i : i + 1] / work[i : i + 1, i : i + 1]
        work = work - jnp.where(rows[:, :1] > i, scale, 0.0) * work[i : i + 1, :]
    diagonal = jnp.sum(jnp.where(rows == lanes, work, 0.0), axis=1, keepdims=True)
    return jnp.where(lanes >= rows, work, 0.0) / jnp.sqrt(diagonal)


def invert(coupling):
    rows = lax.broadcasted_iota(jnp.int32, (PW, PW), 0)
    lanes = lax.broadcasted_iota(jnp.int32, (PW, PW), 1)
    tall = lax.broadcasted_iota(jnp.int32, (PW, 1), 0)
    unit = jnp.where(rows == lanes, 1.0, 0.0).astype(F32)
    work = jnp.concatenate([coupling, unit], axis=1)
    for i in range(PW):
        pivot = work[i : i + 1, :] / work[i : i + 1, i : i + 1]
        work = jnp.where(tall == i, pivot, work - work[:, i : i + 1] * pivot)
    return work[:, PW : 2 * PW]


def basis_of(left, corner_t, first):
    spread = jnp.concatenate([jnp.zeros((PW, PW), F32), corner_t], axis=1)
    wide = lax.broadcasted_iota(jnp.int32, (PW, 2 * PW), 1)
    placed = jnp.where((wide >= PW) & first, spread, left[:, : 2 * PW].astype(F32))
    return jnp.concatenate([placed.astype(BF16), left[:, 2 * PW :]], axis=1)


def exchange(shape, a_hbm, left_out, right_out,
             a, rowp, colp, gpart,
             li, lj, zp, zs, zr, zx, zi, zj, gs, gr, gx, g, kp, ks, kz, kc, kf, kk,
             upper_ref, core_ref,
             a_sem, send_z, send_d, send_y, recv_y, send_x, recv_x, send_k, recv_k,
             recv_b, recv_d, send_c, recv_c):
    nz, nx, ny = shape
    size = a.shape[0]
    row, col = lax.axis_index("row"), lax.axis_index("col")
    z, c = row // 2, row % 2
    x, y = col // ny, col % ny
    partner = (z * 2 + 1 - c, col)

    def at_z(d):
        return (lax.rem(z + d, nz) * 2 + c, col)

    def at_y(d):
        return (row, x * ny + lax.rem(y + d, ny))

    def at_x(d):
        return (row, lax.rem(x + d, nx) * ny + y)

    def to_y(d):
        return lax.rem(y + d, ny)

    def from_y(d):
        return lax.rem(y + ny - d, ny)

    def copy(src, dst, send, recv, where):
        return pltpu.make_async_remote_copy(
            src_ref=src, dst_ref=dst, send_sem=send, recv_sem=recv,
            device_id=where, device_id_type=MESH,
        )

    def got(ref, sem):
        copy(ref, ref, sem, sem, partner).wait_recv()

    def sent(ref, sem):
        copy(ref, ref, sem, sem, partner).wait_send()

    fetch = pltpu.make_async_copy(a_hbm, a, a_sem.at[0])
    fetch.start()
    barrier = pltpu.get_barrier_semaphore()
    peers = [at_z(d) for d in range(1, nz)] + [at_y(d) for d in range(1, ny)]
    peers += [at_x(d) for d in range(1, nx)] + [partner]
    for peer in peers:
        pl.semaphore_signal(barrier, inc=1, device_id=peer, device_id_type=MESH)
    fetch.wait()

    bands = lax.broadcasted_iota(jnp.int32, (2 * PW, size), 0)
    places = lax.broadcasted_iota(jnp.int32, (2 * PW, size), 1)
    hidden = (bands < PW) & (places < PW)

    @pl.when(col == 0)
    def _():
        panel = jnp.where(hidden & (row == 0), 0.0, a[:, : 2 * PW].T)
        rowp[...] = panel.astype(BF16).reshape(rowp.shape)

    @pl.when(row == 0)
    def _():
        panel = jnp.where(hidden & (col == 0), 0.0, a[: 2 * PW, :])
        half = panel.astype(BF16)
        colp[...] = half.reshape(colp.shape)
        lj[...] = half.reshape(colp.shape)
        gram = dot(panel[:PW], panel[:PW], ((1,), (1,)), HIGHEST)
        cross = dot(half[:PW], half[PW:], ((1,), (1,)))
        right = a[PW : 2 * PW, PW : 2 * PW].astype(BF16).astype(F32)
        top = jnp.concatenate([a[PW : 2 * PW, :PW], right], axis=1)
        top = jnp.where(col == 0, top, 0.0)
        whole = jnp.concatenate([jnp.concatenate([gram, cross], axis=1), top], axis=0)
        gpart[...] = whole.reshape(gpart.shape)

    pl.semaphore_wait(barrier, len(peers))

    @pl.when(row == 0)
    def _():
        for d in far_first(nz):
            copy(colp.at[0], lj.at[0], send_z.at[0, d], recv_b.at[0], at_z(d)).start()
        copy(colp.at[0], lj.at[0], send_c.at[0], recv_b.at[0], partner).start()
        for d in far_first(ny):
            copy(gpart.at[to_y(d)], gs.at[d], send_y.at[1, d], recv_y.at[1, d], at_y(d)).start()

    @pl.when(col == 0)
    def _():
        for d in far_first(ny):
            copy(rowp.at[d], li.at[d], send_y.at[0, d], recv_b.at[2], at_y(d)).start()
        for d in range(1, nx):
            copy(rowp.at[0], li.at[0], send_x.at[0, d], recv_x.at[0, 0], at_x(d)).start()
        li[0] = rowp[0]

    @pl.when(row == 0)
    def _():
        total = gpart[y]
        for d in range(1, ny):
            got(gs.at[d], recv_y.at[1, d])
            total += gs[d]
        gr[...] = total
        for d in range(1, nx):
            copy(gr, gx.at[d], send_x.at[1, d], recv_x.at[1, d], at_x(d)).start()

    @pl.when((x == 0) & (y != 0))
    def _():
        got(li.at[y], recv_b.at[2])
        for d in range(1, nx):
            copy(li.at[y], li.at[y], send_x.at[0, d], recv_x.at[0, 0], at_x(d)).start()

    @pl.when(row == 0)
    def _():
        total = gr[...]
        for d in range(1, nx):
            got(gx.at[d], recv_x.at[1, d])
            total += gx[d]
        g[y] = total
        for d in far_first(ny):
            copy(g.at[y], g.at[y], send_y.at[4, d], recv_y.at[4, d], at_y(d)).start()

    @pl.when(x != 0)
    def _():
        got(li.at[y], recv_x.at[0, 0])

    @pl.when(col == 0)
    def _():
        for d in far_first(ny):
            copy(rowp.at[0], li.at[0], send_y.at[2, d], recv_y.at[2, d], at_y(d)).start()

    @pl.when(col != 0)
    def _():
        for d in far_first(ny):
            copy(li.at[y], li.at[y], send_y.at[2, d], recv_y.at[2, d], at_y(d)).start()

    @pl.when((row != 0) & (c == 0))
    def _():
        got(lj.at[0], recv_b.at[0])
        copy(lj.at[0], lj.at[0], send_c.at[0], recv_b.at[0], partner).start()

    @pl.when(c == 1)
    def _():
        got(lj.at[0], recv_b.at[0])

    part = dot(lj[0], a[...].astype(BF16), ((1,), (1,)))
    zp[...] = part.reshape(zp.shape)
    for d in far_first(ny):
        copy(zp.at[to_y(d)], zs.at[d], send_y.at[3, d], recv_y.at[3, d], at_y(d)).start()

    @pl.when(row == 0)
    def _():
        for d in range(1, ny):
            got(g.at[from_y(d)], recv_y.at[4, d])
        for d in far_first(nz):
            copy(g, g, send_z.at[1, d], recv_b.at[1], at_z(d)).start()
        copy(g, g, send_c.at[1], recv_b.at[1], partner).start()
        for d in far_first(nz):
            copy(colp.at[1], lj.at[1], send_z.at[2, d], recv_b.at[3], at_z(d)).start()
        copy(colp.at[1], lj.at[1], send_c.at[2], recv_b.at[3], partner).start()

    total = zp[y]
    for d in range(1, ny):
        got(zs.at[d], recv_y.at[3, d])
        total += zs[d]
    zr[...] = total
    for d in range(1, nx):
        copy(zr, zx.at[d], send_x.at[2, d], recv_x.at[2, d], at_x(d)).start()

    for d in range(1, ny):
        got(li.at[from_y(d)], recv_y.at[2, d])
    panel = li[...].reshape(2 * PW, size)

    for d in range(1, nx):
        got(zx.at[d], recv_x.at[2, d])
        total += zx[d]
    zi[y] = total
    for d in far_first(ny):
        copy(zi.at[y], zi.at[y], send_y.at[5, d], recv_y.at[5, d], at_y(d)).start()

    mine = dot(total, panel.astype(F32), ((1,), (1,)), HIGHEST)
    kp[...] = mine
    for d in far_first(nz):
        copy(kp, ks.at[d], send_k.at[d], recv_k.at[d], at_z(d)).start()

    def forward(d):
        @pl.when(row == col)
        def _():
            there = from_y(d)
            for e in far_first(nz):
                copy(zi.at[there], zj.at[there], send_d.at[d, e], recv_d.at[there], at_z(e)).start()
            copy(zi.at[there], zj.at[there], send_d.at[d, 0], recv_d.at[there], partner).start()

    forward(0)

    @pl.when((row != 0) & (c == 0))
    def _():
        got(g, recv_b.at[1])
        copy(g, g, send_c.at[1], recv_b.at[1], partner).start()

    @pl.when(c == 1)
    def _():
        got(g, recv_b.at[1])

    whole = g[...].reshape(2 * PW, 2 * PW)
    gram, cross = whole[:PW, :PW], whole[:PW, PW:]
    top, top_right = whole[PW:, :PW], whole[PW:, PW:]
    upper_ref[...] = eliminate(gram)

    for d in range(1, ny):
        got(zi.at[from_y(d)], recv_y.at[5, d])
        forward(d)

    for d in range(1, nz):
        got(ks.at[d], recv_k.at[d])
        mine += ks[d]
    kz[...] = mine
    copy(kz, kc, send_c.at[3], recv_c.at[0], partner).start()

    upper = upper_ref[...]
    shifted = top + upper
    core_ref[...] = invert(dot(shifted, upper, ((0,), (0,)), HIGHEST))
    core = core_ref[...]

    got(kc, recv_c.at[0])
    mine += kc[...]
    kf[...] = mine
    for d in far_first(ny):
        copy(kf, kk.at[y], send_y.at[6, d], recv_y.at[6, d], at_y(d)).start()
    kk[y] = mine

    @pl.when((row != 0) & (c == 0))
    def _():
        got(lj.at[1], recv_b.at[3])
        copy(lj.at[1], lj.at[1], send_c.at[2], recv_b.at[3], partner).start()

    corner = shifted.astype(BF16)
    change = corner.astype(F32) - top.astype(BF16).astype(F32)
    corner_t = corner.astype(F32).T
    side = dot(cross, change, ((1,), (0,)), HIGHEST)
    side = side + dot(change, cross, ((0,), (1,)), HIGHEST)
    inner = dot(top_right, change, ((1,), (0,)), HIGHEST)
    side = side + dot(change, inner, ((0,), (0,)), HIGHEST)

    def first_term(right, images):
        full = images + dot(change, right.astype(F32), ((0,), (0,)), HIGHEST)
        return dot(core, full, ((0,), (0,)), HIGHEST)

    basis_i = basis_of(panel[:PW], corner_t, row == 0)
    basis_j = basis_of(lj[0], corner_t, col == 0)
    left_out[:PW, :] = basis_i
    right_out[PW:, :] = basis_j
    first_i = first_term(panel[PW:], zi[...].reshape(PW, size))

    @pl.when((row != col) & (c == col % 2))
    def _():
        for d in range(ny):
            there = d
            got(zj.at[there], recv_d.at[there])
            copy(zj.at[there], zj.at[there], send_d.at[d, 0], recv_d.at[there], partner).start()

    @pl.when(c != col % 2)
    def _():
        for d in range(ny):
            got(zj.at[d], recv_d.at[d])

    @pl.when(c == 1)
    def _():
        got(lj.at[1], recv_b.at[3])

    @pl.when(row == col)
    def _():
        zj[...] = zi[...]

    first_j = first_term(lj[1], zj[...].reshape(PW, size))

    for d in range(1, ny):
        got(kk.at[from_y(d)], recv_y.at[6, d])
    projection = kk[...].reshape(PW, 2 * PW)[:, :PW] + side
    middle = dot(core, projection, ((0,), (0,)), HIGHEST)
    middle = dot(middle, core, ((1,), (0,)), HIGHEST)

    def update_of(first, basis):
        second = dot(middle, basis.astype(F32), ((0,), (0,)), HIGHEST)
        return (first - 0.5 * second).astype(BF16)

    left_out[PW:, :] = update_of(first_i, basis_i)
    right_out[:PW, :] = update_of(first_j, basis_j)

    for d in range(1, ny):
        sent(li.at[0], send_y.at[2, d])
        sent(zr, send_y.at[3, d])
        sent(zr, send_y.at[5, d])
        sent(kp, send_y.at[6, d])
    for d in range(1, nx):
        sent(zr, send_x.at[2, d])
    for d in range(1, nz):
        sent(kp, send_k.at[d])
    sent(kp, send_c.at[3])

    @pl.when(x == 0)
    def _():
        for d in range(1, nx):
            sent(li.at[0], send_x.at[0, d])

    @pl.when(col == 0)
    def _():
        for d in range(1, ny):
            sent(li.at[0], send_y.at[0, d])

    @pl.when(row == 0)
    def _():
        for d in range(1, ny):
            sent(gr, send_y.at[1, d])
            sent(gr, send_y.at[4, d])
        for d in range(1, nx):
            sent(gr, send_x.at[1, d])
        for d in range(1, nz):
            sent(lj.at[0], send_z.at[0, d])
            sent(g, send_z.at[1, d])
            sent(lj.at[1], send_z.at[2, d])

    @pl.when(c == 0)
    def _():
        sent(lj.at[0], send_c.at[0])
        sent(g, send_c.at[1])
        sent(lj.at[1], send_c.at[2])

    @pl.when(c == col % 2)
    def _():
        for d in range(ny):
            sent(zr, send_d.at[d, 0])

    @pl.when(row == col)
    def _():
        for d in range(ny):
            for e in range(1, nz):
                sent(zr, send_d.at[d, e])


def on_device(shape, matrix):
    nz, nx, ny = shape
    size = matrix.shape[0]
    tall, low = 2 * PW // ny, PW // ny
    dma = pltpu.SemaphoreType.DMA
    scratch = [
        pltpu.VMEM((size, size), F32),
        pltpu.VMEM((ny, tall, size), BF16),
        pltpu.VMEM((2, PW, size), BF16),
        pltpu.VMEM((ny, tall, 2 * PW), F32),
        pltpu.VMEM((ny, tall, size), BF16),
        pltpu.VMEM((2, PW, size), BF16),
        pltpu.VMEM((ny, low, size), F32),
        pltpu.VMEM((ny, low, size), F32),
        pltpu.VMEM((low, size), F32),
        pltpu.VMEM((nx, low, size), F32),
        pltpu.VMEM((ny, low, size), F32),
        pltpu.VMEM((ny, low, size), F32),
        pltpu.VMEM((ny, tall, 2 * PW), F32),
        pltpu.VMEM((tall, 2 * PW), F32),
        pltpu.VMEM((nx, tall, 2 * PW), F32),
        pltpu.VMEM((ny, tall, 2 * PW), F32),
        pltpu.VMEM((low, 2 * PW), F32),
        pltpu.VMEM((nz, low, 2 * PW), F32),
        pltpu.VMEM((low, 2 * PW), F32),
        pltpu.VMEM((low, 2 * PW), F32),
        pltpu.VMEM((low, 2 * PW), F32),
        pltpu.VMEM((ny, low, 2 * PW), F32),
        pltpu.VMEM((PW, PW), F32),
        pltpu.VMEM((PW, PW), F32),
        dma((1,)), dma((3, nz)), dma((ny, nz)), dma((7, ny)), dma((7, ny)),
        dma((3, nx)), dma((3, nx)), dma((nz,)), dma((nz,)),
        dma((4,)), dma((ny,)), dma((4,)), dma((1,)),
    ]
    vmem = pl.BlockSpec(memory_space=pltpu.VMEM)
    left, right = pl.pallas_call(
        functools.partial(exchange, shape),
        out_shape=(jax.ShapeDtypeStruct((2 * PW, size), BF16),) * 2,
        in_specs=[pl.BlockSpec(memory_space=pl.ANY)],
        out_specs=(vmem, vmem),
        scratch_shapes=scratch,
        compiler_params=pltpu.CompilerParams(collective_id=0, has_side_effects=True),
        name="exchange",
    )(matrix)
    return matrix - dot(left, right, ((0,), (0,)))


def grid_of(mesh):
    rows, cols = mesh.shape["row"], mesh.shape["col"]
    return {(32, 32): (16, 4, 8), (4, 4): (2, 2, 2)}[(rows, cols)]


def solution(mesh):
    return jax.shard_map(
        functools.partial(on_device, grid_of(mesh)),
        mesh=mesh,
        in_specs=(P("row", "col"),),
        out_specs=P("row", "col"),
        check_vma=False,
    )
```

```python
import functools

import jax
import jax.numpy as jnp
from jax import lax
from jax.experimental import pallas as pl
from jax.experimental.pallas import tpu as pltpu
from jax.sharding import PartitionSpec as P

PW = 64
HIGHEST = lax.Precision.HIGHEST
MESH = pl.DeviceIdType.MESH
F32 = jnp.float32
BF16 = jnp.bfloat16


def dot(first, second, dims, precision=None):
    return lax.dot_general(
        first, second, (dims, ((), ())), precision=precision, preferred_element_type=F32
    )


def far_first(count):
    return sorted(range(1, count), key=lambda d: -min(d, count - d))


def eliminate(gram):
    rows = lax.broadcasted_iota(jnp.int32, (PW, PW), 0)
    lanes = lax.broadcasted_iota(jnp.int32, (PW, PW), 1)
    unit = jnp.where(rows == lanes, 1.0, 0.0).astype(F32)
    work = jnp.concatenate([gram, unit], axis=1)
    for i in range(PW):
        scale = work[:, i : i + 1] / work[i : i + 1, i : i + 1]
        work = work - jnp.where(rows[:, :1] > i, scale, 0.0) * work[i : i + 1, :]
    upper, lower = work[:, :PW], work[:, PW:]
    diagonal = jnp.sum(jnp.where(rows == lanes, upper, 0.0), axis=1, keepdims=True)
    root = jnp.sqrt(diagonal)
    return jnp.where(lanes >= rows, upper, 0.0) / root, jnp.where(lanes <= rows, lower, 0.0) / root


def invert(coupling):
    rows = lax.broadcasted_iota(jnp.int32, (PW, PW), 0)
    lanes = lax.broadcasted_iota(jnp.int32, (PW, PW), 1)
    tall = lax.broadcasted_iota(jnp.int32, (PW, 1), 0)
    unit = jnp.where(rows == lanes, 1.0, 0.0).astype(F32)
    work = jnp.concatenate([coupling, unit], axis=1)
    for i in range(PW):
        pivot = work[i : i + 1, :] / work[i : i + 1, i : i + 1]
        work = jnp.where(tall == i, pivot, work - work[:, i : i + 1] * pivot)
    return work[:, PW : 2 * PW]


def basis_of(left, corner_t, first):
    spread = jnp.concatenate([jnp.zeros((PW, PW), F32), corner_t], axis=1)
    wide = lax.broadcasted_iota(jnp.int32, (PW, 2 * PW), 1)
    placed = jnp.where((wide >= PW) & first, spread, left[:, : 2 * PW].astype(F32))
    return jnp.concatenate([placed.astype(BF16), left[:, 2 * PW :]], axis=1)


def exchange(shape, a_hbm, left_out, right_out,
             a, rowp, colp, gpart,
             li, lj, zp, zs, zr, zx, zi, zh, zj, gs, gr, gx, g, kp, ks, kz, kc, kf, kk,
             a_sem, send_z, send_d, send_y, recv_y, send_x, recv_x, send_k, recv_k,
             recv_b, send_c, recv_c):
    nz, nx, ny = shape
    size = a.shape[0]
    row, col = lax.axis_index("row"), lax.axis_index("col")
    z, c = row // 2, row % 2
    x, y = col // ny, col % ny
    partner = (z * 2 + 1 - c, col)

    def at_z(d):
        return (lax.rem(z + d, nz) * 2 + c, col)

    def at_y(d):
        return (row, x * ny + lax.rem(y + d, ny))

    def at_x(d):
        return (row, lax.rem(x + d, nx) * ny + y)

    def to_y(d):
        return lax.rem(y + d, ny)

    def from_y(d):
        return lax.rem(y + ny - d, ny)

    def copy(src, dst, send, recv, where):
        return pltpu.make_async_remote_copy(
            src_ref=src, dst_ref=dst, send_sem=send, recv_sem=recv,
            device_id=where, device_id_type=MESH,
        )

    def got(ref, sem):
        copy(ref, ref, sem, sem, partner).wait_recv()

    def sent(ref, sem):
        copy(ref, ref, sem, sem, partner).wait_send()

    fetch = pltpu.make_async_copy(a_hbm, a, a_sem.at[0])
    fetch.start()
    barrier = pltpu.get_barrier_semaphore()
    peers = [at_z(d) for d in range(1, nz)] + [at_y(d) for d in range(1, ny)]
    peers += [at_x(d) for d in range(1, nx)] + [partner]
    for peer in peers:
        pl.semaphore_signal(barrier, inc=1, device_id=peer, device_id_type=MESH)
    fetch.wait()

    bands = lax.broadcasted_iota(jnp.int32, (2 * PW, size), 0)
    places = lax.broadcasted_iota(jnp.int32, (2 * PW, size), 1)
    hidden = (bands < PW) & (places < PW)

    @pl.when(col == 0)
    def _():
        panel = jnp.where(hidden & (row == 0), 0.0, a[:, : 2 * PW].T)
        rowp[...] = panel.astype(BF16).reshape(rowp.shape)

    @pl.when(row == 0)
    def _():
        panel = jnp.where(hidden & (col == 0), 0.0, a[: 2 * PW, :])
        half = panel.astype(BF16)
        colp[...] = half.reshape(colp.shape)
        lj[...] = half.reshape(colp.shape)
        gram = dot(panel[:PW], panel[:PW], ((1,), (1,)), HIGHEST)
        cross = dot(half[:PW], half[PW:], ((1,), (1,)))
        right = a[PW : 2 * PW, PW : 2 * PW].astype(BF16).astype(F32)
        top = jnp.concatenate([a[PW : 2 * PW, :PW], right], axis=1)
        top = jnp.where(col == 0, top, 0.0)
        whole = jnp.concatenate([jnp.concatenate([gram, cross], axis=1), top], axis=0)
        gpart[...] = whole.reshape(gpart.shape)

    pl.semaphore_wait(barrier, len(peers))

    @pl.when(row == 0)
    def _():
        for d in far_first(nz):
            copy(colp.at[0], lj.at[0], send_z.at[0, d], recv_b.at[0], at_z(d)).start()
        copy(colp.at[0], lj.at[0], send_c.at[0], recv_b.at[0], partner).start()
        for d in far_first(ny):
            copy(gpart.at[to_y(d)], gs.at[d], send_y.at[1, d], recv_y.at[1, d], at_y(d)).start()

    @pl.when(col == 0)
    def _():
        for d in far_first(ny):
            copy(rowp.at[d], li.at[d], send_y.at[0, d], recv_b.at[2], at_y(d)).start()
        for d in range(1, nx):
            copy(rowp.at[0], li.at[0], send_x.at[0, d], recv_x.at[0, 0], at_x(d)).start()
        li[0] = rowp[0]

    @pl.when(row == 0)
    def _():
        total = gpart[y]
        for d in range(1, ny):
            got(gs.at[d], recv_y.at[1, d])
            total += gs[d]
        gr[...] = total
        for d in range(1, nx):
            copy(gr, gx.at[d], send_x.at[1, d], recv_x.at[1, d], at_x(d)).start()

    @pl.when((x == 0) & (y != 0))
    def _():
        got(li.at[y], recv_b.at[2])
        for d in range(1, nx):
            copy(li.at[y], li.at[y], send_x.at[0, d], recv_x.at[0, 0], at_x(d)).start()

    @pl.when(row == 0)
    def _():
        total = gr[...]
        for d in range(1, nx):
            got(gx.at[d], recv_x.at[1, d])
            total += gx[d]
        g[y] = total
        for d in far_first(ny):
            copy(g.at[y], g.at[y], send_y.at[4, d], recv_y.at[4, d], at_y(d)).start()

    @pl.when(x != 0)
    def _():
        got(li.at[y], recv_x.at[0, 0])

    @pl.when(col == 0)
    def _():
        for d in far_first(ny):
            copy(rowp.at[0], li.at[0], send_y.at[2, d], recv_y.at[2, d], at_y(d)).start()

    @pl.when(col != 0)
    def _():
        for d in far_first(ny):
            copy(li.at[y], li.at[y], send_y.at[2, d], recv_y.at[2, d], at_y(d)).start()

    @pl.when((row != 0) & (c == 0))
    def _():
        got(lj.at[0], recv_b.at[0])
        copy(lj.at[0], lj.at[0], send_c.at[0], recv_b.at[0], partner).start()

    @pl.when(c == 1)
    def _():
        got(lj.at[0], recv_b.at[0])

    part = dot(lj[0], a[...].astype(BF16), ((1,), (1,)))
    zp[...] = part.reshape(zp.shape)
    for d in far_first(ny):
        copy(zp.at[to_y(d)], zs.at[d], send_y.at[3, d], recv_y.at[3, d], at_y(d)).start()

    @pl.when(row == 0)
    def _():
        for d in range(1, ny):
            got(g.at[from_y(d)], recv_y.at[4, d])
        for d in far_first(nz):
            copy(g, g, send_z.at[1, d], recv_b.at[1], at_z(d)).start()
        copy(g, g, send_c.at[1], recv_b.at[1], partner).start()
        for d in far_first(nz):
            copy(colp.at[1], lj.at[1], send_z.at[2, d], recv_b.at[3], at_z(d)).start()
        copy(colp.at[1], lj.at[1], send_c.at[2], recv_b.at[3], partner).start()

    total = zp[y]
    for d in range(1, ny):
        got(zs.at[d], recv_y.at[3, d])
        total += zs[d]
    zr[...] = total
    for d in range(1, nx):
        copy(zr, zx.at[d], send_x.at[2, d], recv_x.at[2, d], at_x(d)).start()

    for d in range(1, ny):
        got(li.at[from_y(d)], recv_y.at[2, d])
    panel = li[...].reshape(2 * PW, size)

    for d in range(1, nx):
        got(zx.at[d], recv_x.at[2, d])
        total += zx[d]
    zi[y] = total
    for d in far_first(ny):
        copy(zi.at[y], zi.at[y], send_y.at[5, d], recv_y.at[5, d], at_y(d)).start()

    mine = dot(total, panel.astype(F32), ((1,), (1,)), HIGHEST)
    kp[...] = mine
    for d in far_first(nz):
        copy(kp, ks.at[d], send_k.at[d], recv_k.at[d], at_z(d)).start()

    @pl.when((row != 0) & (c == 0))
    def _():
        got(g, recv_b.at[1])
        copy(g, g, send_c.at[1], recv_b.at[1], partner).start()

    @pl.when(c == 1)
    def _():
        got(g, recv_b.at[1])

    whole = g[...].reshape(2 * PW, 2 * PW)
    gram, cross = whole[:PW, :PW], whole[:PW, PW:]
    top, top_right = whole[PW:, :PW], whole[PW:, PW:]
    upper, inverse_t = eliminate(gram)

    for d in range(1, ny):
        got(zi.at[from_y(d)], recv_y.at[5, d])
    images = zi[...].reshape(PW, size)

    @pl.when(row == col)
    def _():
        half = dot(inverse_t, images, ((1,), (0,)), HIGHEST).astype(BF16)
        zh[...] = half
        zj[...] = half
        for d in far_first(nz):
            copy(zh, zj, send_d.at[d], recv_b.at[4], at_z(d)).start()
        copy(zh, zj, send_d.at[0], recv_b.at[4], partner).start()

    for d in range(1, nz):
        got(ks.at[d], recv_k.at[d])
        mine += ks[d]
    kz[...] = mine
    copy(kz, kc, send_c.at[3], recv_c.at[0], partner).start()

    shifted = top + upper
    coupling = dot(shifted, upper, ((0,), (0,)), HIGHEST)
    corner = shifted.astype(BF16)
    change = corner.astype(F32) - top.astype(BF16).astype(F32)
    side = dot(cross, change, ((1,), (0,)), HIGHEST)
    side = side + dot(change, cross, ((0,), (1,)), HIGHEST)
    inner = dot(top_right, change, ((1,), (0,)), HIGHEST)
    side = side + dot(change, inner, ((0,), (0,)), HIGHEST)

    got(kc, recv_c.at[0])
    mine += kc[...]
    kf[...] = mine
    for d in far_first(ny):
        copy(kf, kk.at[y], send_y.at[6, d], recv_y.at[6, d], at_y(d)).start()
    kk[y] = mine

    @pl.when((row != 0) & (c == 0))
    def _():
        got(lj.at[1], recv_b.at[3])
        copy(lj.at[1], lj.at[1], send_c.at[2], recv_b.at[3], partner).start()

    @pl.when(c == 1)
    def _():
        got(lj.at[1], recv_b.at[3])

    core = invert(coupling)
    corner_t = corner.astype(F32).T
    basis_i = basis_of(panel[:PW], corner_t, row == 0).astype(F32).T
    basis_j = basis_of(lj[0], corner_t, col == 0)
    right_out[PW:, :] = basis_j
    shift = dot(change, core, ((1,), (0,)), HIGHEST)
    first_i = dot(core, images, ((0,), (0,)), HIGHEST)
    first_i = first_i + dot(shift, panel[PW:].astype(F32), ((0,), (0,)), HIGHEST)
    first_i = first_i.T
    shift_j = dot(shift, lj[1].astype(F32), ((0,), (0,)), HIGHEST)
    scaled = dot(upper, core, ((1,), (0,)), HIGHEST)

    for d in range(1, ny):
        got(kk.at[from_y(d)], recv_y.at[6, d])
    projection = kk[...].reshape(PW, 2 * PW)[:, :PW] + side
    middle = dot(core, projection, ((0,), (0,)), HIGHEST)
    middle = 0.5 * dot(middle, core, ((1,), (0,)), HIGHEST)
    update_i = first_i - dot(basis_i, middle, ((1,), (0,)), HIGHEST)
    left_out[...] = jnp.concatenate([basis_i, update_i], axis=1).astype(BF16)
    shift_j = shift_j - dot(middle, basis_j.astype(F32), ((0,), (0,)), HIGHEST)

    @pl.when((row != col) & (c == col % 2))
    def _():
        got(zj, recv_b.at[4])
        copy(zj, zj, send_d.at[0], recv_b.at[4], partner).start()

    @pl.when(c != col % 2)
    def _():
        got(zj, recv_b.at[4])

    first_j = dot(scaled, zj[...].astype(F32), ((0,), (0,)), HIGHEST)
    right_out[:PW, :] = (first_j + shift_j).astype(BF16)

    for d in range(1, ny):
        sent(li.at[0], send_y.at[2, d])
        sent(zr, send_y.at[3, d])
        sent(zr, send_y.at[5, d])
        sent(kp, send_y.at[6, d])
    for d in range(1, nx):
        sent(zr, send_x.at[2, d])
    for d in range(1, nz):
        sent(kp, send_k.at[d])
    sent(kp, send_c.at[3])

    @pl.when(x == 0)
    def _():
        for d in range(1, nx):
            sent(li.at[0], send_x.at[0, d])

    @pl.when(col == 0)
    def _():
        for d in range(1, ny):
            sent(li.at[0], send_y.at[0, d])

    @pl.when(row == 0)
    def _():
        for d in range(1, ny):
            sent(gr, send_y.at[1, d])
            sent(gr, send_y.at[4, d])
        for d in range(1, nx):
            sent(gr, send_x.at[1, d])
        for d in range(1, nz):
            sent(lj.at[0], send_z.at[0, d])
            sent(g, send_z.at[1, d])
            sent(lj.at[1], send_z.at[2, d])

    @pl.when(c == 0)
    def _():
        sent(lj.at[0], send_c.at[0])
        sent(g, send_c.at[1])
        sent(lj.at[1], send_c.at[2])

    @pl.when(c == col % 2)
    def _():
        sent(zh, send_d.at[0])

    @pl.when(row == col)
    def _():
        for d in range(1, nz):
            sent(zh, send_d.at[d])


def on_device(shape, matrix):
    nz, nx, ny = shape
    size = matrix.shape[0]
    tall, low = 2 * PW // ny, PW // ny
    dma = pltpu.SemaphoreType.DMA
    scratch = [
        pltpu.VMEM((size, size), F32),
        pltpu.VMEM((ny, tall, size), BF16),
        pltpu.VMEM((2, PW, size), BF16),
        pltpu.VMEM((ny, tall, 2 * PW), F32),
        pltpu.VMEM((ny, tall, size), BF16),
        pltpu.VMEM((2, PW, size), BF16),
        pltpu.VMEM((ny, low, size), F32),
        pltpu.VMEM((ny, low, size), F32),
        pltpu.VMEM((low, size), F32),
        pltpu.VMEM((nx, low, size), F32),
        pltpu.VMEM((ny, low, size), F32),
        pltpu.VMEM((PW, size), BF16),
        pltpu.VMEM((PW, size), BF16),
        pltpu.VMEM((ny, tall, 2 * PW), F32),
        pltpu.VMEM((tall, 2 * PW), F32),
        pltpu.VMEM((nx, tall, 2 * PW), F32),
        pltpu.VMEM((ny, tall, 2 * PW), F32),
        pltpu.VMEM((low, 2 * PW), F32),
        pltpu.VMEM((nz, low, 2 * PW), F32),
        pltpu.VMEM((low, 2 * PW), F32),
        pltpu.VMEM((low, 2 * PW), F32),
        pltpu.VMEM((low, 2 * PW), F32),
        pltpu.VMEM((ny, low, 2 * PW), F32),
        dma((1,)), dma((3, nz)), dma((nz,)), dma((7, ny)), dma((7, ny)),
        dma((3, nx)), dma((3, nx)), dma((nz,)), dma((nz,)),
        dma((5,)), dma((4,)), dma((1,)),
    ]
    vmem = pl.BlockSpec(memory_space=pltpu.VMEM)
    left, right = pl.pallas_call(
        functools.partial(exchange, shape),
        out_shape=(
            jax.ShapeDtypeStruct((size, 2 * PW), BF16),
            jax.ShapeDtypeStruct((2 * PW, size), BF16),
        ),
        in_specs=[pl.BlockSpec(memory_space=pl.ANY)],
        out_specs=(vmem, vmem),
        scratch_shapes=scratch,
        compiler_params=pltpu.CompilerParams(collective_id=0, has_side_effects=True),
        name="exchange",
    )(matrix)
    return matrix - dot(left, right, ((1,), (0,)))


def grid_of(mesh):
    rows, cols = mesh.shape["row"], mesh.shape["col"]
    return {(32, 32): (16, 4, 8), (4, 4): (2, 2, 2)}[(rows, cols)]


def solution(mesh):
    return jax.shard_map(
        functools.partial(on_device, grid_of(mesh)),
        mesh=mesh,
        in_specs=(P("row", "col"),),
        out_specs=P("row", "col"),
        check_vma=False,
    )
```

```python
import functools

import jax
import jax.numpy as jnp
from jax import lax
from jax.experimental import pallas as pl
from jax.experimental.pallas import tpu as pltpu
from jax.sharding import PartitionSpec as P

PW = 64
HIGHEST = lax.Precision.HIGHEST
MESH = pl.DeviceIdType.MESH
F32 = jnp.float32
BF16 = jnp.bfloat16


def dot(first, second, dims, precision=None):
    return lax.dot_general(
        first, second, (dims, ((), ())), precision=precision, preferred_element_type=F32
    )


def far_first(count):
    return sorted(range(1, count), key=lambda d: -min(d, count - d))


def two_columns(work, i):
    first = jnp.broadcast_to(work[:, i : i + 1], work.shape)
    second = jnp.broadcast_to(work[:, i + 1 : i + 2], work.shape)
    return first, second


def eliminate(gram):
    rows = lax.broadcasted_iota(jnp.int32, (PW, PW), 0)
    lanes = lax.broadcasted_iota(jnp.int32, (PW, PW), 1)
    tall = lax.broadcasted_iota(jnp.int32, (PW, 2 * PW), 0)
    unit = jnp.where(rows == lanes, 1.0, 0.0).astype(F32)
    work = jnp.concatenate([gram, unit], axis=1)
    for i in range(0, PW, 2):
        first, second = two_columns(work, i)
        a, b = first[i : i + 1], second[i : i + 1]
        e, d = first[i + 1 : i + 2], second[i + 1 : i + 2]
        over_a = 1.0 / a
        over_q = a / (a * d - b * e)
        scaled = first * over_a
        rest = (second - scaled * b) * over_q
        top, low = work[i : i + 1], work[i + 1 : i + 2]
        low = low - (e * over_a) * top
        work = work - jnp.where(tall > i, scaled, 0.0) * top
        work = work - jnp.where(tall > i + 1, rest, 0.0) * low
    upper, lower = work[:, :PW], work[:, PW:]
    diagonal = jnp.sum(jnp.where(rows == lanes, upper, 0.0), axis=1, keepdims=True)
    root = 1.0 / jnp.sqrt(diagonal)
    return jnp.where(lanes >= rows, upper, 0.0) * root, jnp.where(lanes <= rows, lower, 0.0) * root


def invert(coupling):
    rows = lax.broadcasted_iota(jnp.int32, (PW, PW), 0)
    lanes = lax.broadcasted_iota(jnp.int32, (PW, PW), 1)
    tall = lax.broadcasted_iota(jnp.int32, (PW, 2 * PW), 0)
    unit = jnp.where(rows == lanes, 1.0, 0.0).astype(F32)
    work = jnp.concatenate([coupling, unit], axis=1)
    for i in range(0, PW, 2):
        first, second = two_columns(work, i)
        a, b = first[i : i + 1], second[i : i + 1]
        e, d = first[i + 1 : i + 2], second[i + 1 : i + 2]
        over = 1.0 / (a * d - b * e)
        top, low = work[i : i + 1], work[i + 1 : i + 2]
        new_top = (d * over) * top - (b * over) * low
        new_low = (a * over) * low - (e * over) * top
        work = work - first * new_top - second * new_low
        work = jnp.where(tall == i, new_top, jnp.where(tall == i + 1, new_low, work))
    return work[:, PW : 2 * PW]


def basis_of(left, corner_t, first):
    spread = jnp.concatenate([jnp.zeros((PW, PW), F32), corner_t], axis=1)
    wide = lax.broadcasted_iota(jnp.int32, (PW, 2 * PW), 1)
    placed = jnp.where((wide >= PW) & first, spread, left[:, : 2 * PW].astype(F32))
    return jnp.concatenate([placed.astype(BF16), left[:, 2 * PW :]], axis=1)


def exchange(shape, a_hbm, left_out, right_out,
             a, rowp, colp, gpart,
             li, lj, zp, zs, zr, zx, zi, zh, zj, gs, gr, gx, g, kp, ks, kz, kc, kf, kk,
             a_sem, send_z, send_d, send_y, recv_y, send_x, recv_x, send_k, recv_k,
             recv_b, send_c, recv_c):
    nz, nx, ny = shape
    size = a.shape[0]
    row, col = lax.axis_index("row"), lax.axis_index("col")
    z, c = row // 2, row % 2
    x, y = col // ny, col % ny
    partner = (z * 2 + 1 - c, col)

    def at_z(d):
        return (lax.rem(z + d, nz) * 2 + c, col)

    def at_y(d):
        return (row, x * ny + lax.rem(y + d, ny))

    def at_x(d):
        return (row, lax.rem(x + d, nx) * ny + y)

    def to_y(d):
        return lax.rem(y + d, ny)

    def from_y(d):
        return lax.rem(y + ny - d, ny)

    def copy(src, dst, send, recv, where):
        return pltpu.make_async_remote_copy(
            src_ref=src, dst_ref=dst, send_sem=send, recv_sem=recv,
            device_id=where, device_id_type=MESH,
        )

    def got(ref, sem):
        copy(ref, ref, sem, sem, partner).wait_recv()

    def sent(ref, sem):
        copy(ref, ref, sem, sem, partner).wait_send()

    fetch = pltpu.make_async_copy(a_hbm, a, a_sem.at[0])
    fetch.start()
    barrier = pltpu.get_barrier_semaphore()
    peers = [at_z(d) for d in range(1, nz)] + [at_y(d) for d in range(1, ny)]
    peers += [at_x(d) for d in range(1, nx)] + [partner]
    for peer in peers:
        pl.semaphore_signal(barrier, inc=1, device_id=peer, device_id_type=MESH)
    fetch.wait()

    bands = lax.broadcasted_iota(jnp.int32, (2 * PW, size), 0)
    places = lax.broadcasted_iota(jnp.int32, (2 * PW, size), 1)
    hidden = (bands < PW) & (places < PW)

    @pl.when(col == 0)
    def _():
        panel = jnp.where(hidden & (row == 0), 0.0, a[:, : 2 * PW].T)
        rowp[...] = panel.astype(BF16).reshape(rowp.shape)

    @pl.when(row == 0)
    def _():
        panel = jnp.where(hidden & (col == 0), 0.0, a[: 2 * PW, :])
        half = panel.astype(BF16)
        colp[...] = half.reshape(colp.shape)
        lj[...] = half.reshape(colp.shape)
        gram = dot(panel[:PW], panel[:PW], ((1,), (1,)), HIGHEST)
        cross = dot(half[:PW], half[PW:], ((1,), (1,)))
        right = a[PW : 2 * PW, PW : 2 * PW].astype(BF16).astype(F32)
        top = jnp.concatenate([a[PW : 2 * PW, :PW], right], axis=1)
        top = jnp.where(col == 0, top, 0.0)
        whole = jnp.concatenate([jnp.concatenate([gram, cross], axis=1), top], axis=0)
        gpart[...] = whole.reshape(gpart.shape)

    pl.semaphore_wait(barrier, len(peers))

    @pl.when(row == 0)
    def _():
        for d in far_first(nz):
            copy(colp.at[0], lj.at[0], send_z.at[0, d], recv_b.at[0], at_z(d)).start()
        copy(colp.at[0], lj.at[0], send_c.at[0], recv_b.at[0], partner).start()
        for d in far_first(ny):
            copy(gpart.at[to_y(d)], gs.at[d], send_y.at[1, d], recv_y.at[1, d], at_y(d)).start()
        for d in far_first(nz):
            copy(colp.at[1], lj.at[1], send_z.at[2, d], recv_b.at[3], at_z(d)).start()
        copy(colp.at[1], lj.at[1], send_c.at[2], recv_b.at[3], partner).start()

    @pl.when(col == 0)
    def _():
        for d in far_first(ny):
            copy(rowp.at[d], li.at[d], send_y.at[0, d], recv_b.at[2], at_y(d)).start()
        for d in range(1, nx):
            copy(rowp.at[0], li.at[0], send_x.at[0, d], recv_x.at[0, 0], at_x(d)).start()
        li[0] = rowp[0]

    @pl.when(row == 0)
    def _():
        total = gpart[y]
        for d in range(1, ny):
            got(gs.at[d], recv_y.at[1, d])
            total += gs[d]
        gr[...] = total
        for d in range(1, nx):
            copy(gr, gx.at[d], send_x.at[1, d], recv_x.at[1, d], at_x(d)).start()

    @pl.when((x == 0) & (y != 0))
    def _():
        got(li.at[y], recv_b.at[2])
        for d in range(1, nx):
            copy(li.at[y], li.at[y], send_x.at[0, d], recv_x.at[0, 0], at_x(d)).start()

    @pl.when(row == 0)
    def _():
        total = gr[...]
        for d in range(1, nx):
            got(gx.at[d], recv_x.at[1, d])
            total += gx[d]
        g[y] = total
        for d in far_first(ny):
            copy(g.at[y], g.at[y], send_y.at[4, d], recv_y.at[4, d], at_y(d)).start()

    @pl.when(x != 0)
    def _():
        got(li.at[y], recv_x.at[0, 0])

    def hand_out(which):
        @pl.when(which)
        def _():
            for d in far_first(ny):
                copy(li.at[y], li.at[y], send_y.at[2, d], recv_y.at[2, d], at_y(d)).start()

    @pl.when(col == 0)
    def _():
        for d in far_first(ny):
            copy(rowp.at[0], li.at[0], send_y.at[2, d], recv_y.at[2, d], at_y(d)).start()

    hand_out((col != 0) & (y < ny // 2))

    @pl.when((row != 0) & (c == 0))
    def _():
        got(lj.at[0], recv_b.at[0])
        copy(lj.at[0], lj.at[0], send_c.at[0], recv_b.at[0], partner).start()

    @pl.when(c == 1)
    def _():
        got(lj.at[0], recv_b.at[0])

    part = dot(lj[0], a[...].astype(BF16), ((1,), (1,)))
    zp[...] = part.reshape(zp.shape)
    for d in far_first(ny):
        copy(zp.at[to_y(d)], zs.at[d], send_y.at[3, d], recv_y.at[3, d], at_y(d)).start()

    @pl.when(row == 0)
    def _():
        for d in range(1, ny):
            got(g.at[from_y(d)], recv_y.at[4, d])
        for d in far_first(nz):
            copy(g, g, send_z.at[1, d], recv_b.at[1], at_z(d)).start()
        copy(g, g, send_c.at[1], recv_b.at[1], partner).start()

    total = zp[y]
    for d in range(1, ny):
        got(zs.at[d], recv_y.at[3, d])
        total += zs[d]
    zr[...] = total
    for d in range(1, nx):
        copy(zr, zx.at[d], send_x.at[2, d], recv_x.at[2, d], at_x(d)).start()

    hand_out(y >= ny // 2)

    def panel_from(upper_half):
        for d in range(1, ny):
            there = from_y(d)

            @pl.when((there >= ny // 2) == upper_half)
            def _():
                got(li.at[there], recv_y.at[2, d])

    panel_from(False)
    panel_l = li[: ny // 2].reshape(PW, size)

    for d in range(1, nx):
        got(zx.at[d], recv_x.at[2, d])
        total += zx[d]
    zi[y] = total
    for d in far_first(ny):
        copy(zi.at[y], zi.at[y], send_y.at[5, d], recv_y.at[5, d], at_y(d)).start()

    mine = dot(total, panel_l.astype(F32), ((1,), (1,)), HIGHEST)
    mine = jnp.concatenate([mine, mine], axis=1)
    kp[...] = mine
    for d in far_first(nz):
        copy(kp, ks.at[d], send_k.at[d], recv_k.at[d], at_z(d)).start()

    @pl.when((row != 0) & (c == 0))
    def _():
        got(lj.at[1], recv_b.at[3])
        copy(lj.at[1], lj.at[1], send_c.at[2], recv_b.at[3], partner).start()

    @pl.when((row != 0) & (c == 0))
    def _():
        got(g, recv_b.at[1])
        copy(g, g, send_c.at[1], recv_b.at[1], partner).start()

    @pl.when(c == 1)
    def _():
        got(g, recv_b.at[1])

    whole = g[...].reshape(2 * PW, 2 * PW)
    gram, top = whole[:PW, :PW], whole[PW:, :PW]
    rows = lax.broadcasted_iota(jnp.int32, (PW, PW), 0)
    lanes = lax.broadcasted_iota(jnp.int32, (PW, PW), 1)
    on_diagonal = jnp.where(rows == lanes, gram, 0.0)
    diagonal = jnp.sum(on_diagonal, axis=0, keepdims=True)
    across = 1.0 / jnp.sqrt(diagonal)
    down = 1.0 / jnp.sqrt(jnp.sum(on_diagonal, axis=1, keepdims=True))
    unit_upper, inverse_t = eliminate(gram * down * across)
    upper = unit_upper * (diagonal * across)
    inverse_t = inverse_t * across

    for d in range(1, ny):
        got(zi.at[from_y(d)], recv_y.at[5, d])
    images = zi[...].reshape(PW, size)

    @pl.when(row == col)
    def _():
        half = dot(inverse_t, images, ((1,), (0,)), HIGHEST).astype(BF16)
        zh[...] = half
        zj[...] = half
        for d in far_first(nz):
            copy(zh, zj, send_d.at[d], recv_b.at[4], at_z(d)).start()
        copy(zh, zj, send_d.at[0], recv_b.at[4], partner).start()

    for d in range(1, nz):
        got(ks.at[d], recv_k.at[d])
        mine += ks[d]
    kz[...] = mine
    copy(kz, kc, send_c.at[3], recv_c.at[0], partner).start()

    got(kc, recv_c.at[0])
    mine += kc[...]
    kf[...] = mine
    for d in far_first(ny):
        copy(kf, kk.at[y], send_y.at[6, d], recv_y.at[6, d], at_y(d)).start()
    kk[y] = mine

    shifted = top + upper
    coupling = dot(shifted * across, unit_upper, ((0,), (0,)), HIGHEST)
    core = invert(coupling) * down * across
    corner = shifted.astype(BF16)
    change = corner.astype(F32) - top.astype(BF16).astype(F32)
    corner_t = corner.astype(F32).T
    inner = dot(whole[:, PW:], change, ((1,), (0,)), HIGHEST)
    side = inner[:PW] + inner[:PW].T + dot(change, inner[PW:], ((0,), (0,)), HIGHEST)
    mixed = dot(jnp.concatenate([upper, change], axis=0), core, ((1,), (0,)), HIGHEST)

    panel_from(True)
    panel_t = li[ny // 2 :].reshape(PW, size)

    @pl.when(c == 1)
    def _():
        got(lj.at[1], recv_b.at[3])

    basis_i = basis_of(panel_l, corner_t, row == 0)
    basis_j = basis_of(lj[0], corner_t, col == 0)
    left_out[:, :PW] = basis_i.T
    right_out[PW:, :] = basis_j
    high = images.astype(BF16)
    low = (images - high.astype(F32)).astype(BF16)
    stack_i = jnp.concatenate([high, low, panel_t, basis_i], axis=0)
    stack_tb = jnp.concatenate([lj[1], basis_j], axis=0)

    @pl.when((row != col) & (c == col % 2))
    def _():
        got(zj, recv_b.at[4])
        copy(zj, zj, send_d.at[0], recv_b.at[4], partner).start()

    for d in range(1, ny):
        got(kk.at[from_y(d)], recv_y.at[6, d])
    projection = kk[...].reshape(PW, 2 * PW)[:, :PW] + side
    middle = dot(core, projection, ((0,), (0,)), HIGHEST)
    middle = -0.5 * dot(middle, core, ((1,), (0,)), HIGHEST)

    def weigh(weights, stack):
        tall = weights.T
        first = tall.astype(BF16)
        rest = tall - first.astype(F32)
        second = rest.astype(BF16)
        third = (rest - second.astype(F32)).astype(BF16)
        parts = dot(jnp.concatenate([first, second, third], axis=0), stack, ((1,), (0,)))
        return (parts[:PW] + (parts[PW : 2 * PW] + parts[2 * PW :])).astype(BF16)

    weights_i = jnp.concatenate([core, core, mixed[PW:], middle], axis=0)
    left_out[:, PW:] = weigh(weights_i, stack_i).T

    @pl.when(c != col % 2)
    def _():
        got(zj, recv_b.at[4])

    weights_j = jnp.concatenate([mixed, middle], axis=0)
    right_out[:PW, :] = weigh(weights_j, jnp.concatenate([zj[...], stack_tb], axis=0))

    for d in range(1, ny):
        sent(li.at[0], send_y.at[2, d])
        sent(zr, send_y.at[3, d])
        sent(zr, send_y.at[5, d])
        sent(kp, send_y.at[6, d])
    for d in range(1, nx):
        sent(zr, send_x.at[2, d])
    for d in range(1, nz):
        sent(kp, send_k.at[d])
    sent(kp, send_c.at[3])

    @pl.when(x == 0)
    def _():
        for d in range(1, nx):
            sent(li.at[0], send_x.at[0, d])

    @pl.when(col == 0)
    def _():
        for d in range(1, ny):
            sent(li.at[0], send_y.at[0, d])

    @pl.when(row == 0)
    def _():
        for d in range(1, ny):
            sent(gr, send_y.at[1, d])
            sent(gr, send_y.at[4, d])
        for d in range(1, nx):
            sent(gr, send_x.at[1, d])
        for d in range(1, nz):
            sent(lj.at[0], send_z.at[0, d])
            sent(g, send_z.at[1, d])
            sent(lj.at[1], send_z.at[2, d])

    @pl.when(c == 0)
    def _():
        sent(lj.at[0], send_c.at[0])
        sent(g, send_c.at[1])
        sent(lj.at[1], send_c.at[2])

    @pl.when(c == col % 2)
    def _():
        sent(zh, send_d.at[0])

    @pl.when(row == col)
    def _():
        for d in range(1, nz):
            sent(zh, send_d.at[d])


def subtract(a_ref, left_ref, right_ref, out_ref):
    out_ref[...] = a_ref[...] - dot(left_ref[...], right_ref[...], ((1,), (0,)))


def on_device(shape, matrix):
    nz, nx, ny = shape
    size = matrix.shape[0]
    tall, low = 2 * PW // ny, PW // ny
    dma = pltpu.SemaphoreType.DMA
    scratch = [
        pltpu.VMEM((size, size), F32),
        pltpu.VMEM((ny, tall, size), BF16),
        pltpu.VMEM((2, PW, size), BF16),
        pltpu.VMEM((ny, tall, 2 * PW), F32),
        pltpu.VMEM((ny, tall, size), BF16),
        pltpu.VMEM((2, PW, size), BF16),
        pltpu.VMEM((ny, low, size), F32),
        pltpu.VMEM((ny, low, size), F32),
        pltpu.VMEM((low, size), F32),
        pltpu.VMEM((nx, low, size), F32),
        pltpu.VMEM((ny, low, size), F32),
        pltpu.VMEM((PW, size), BF16),
        pltpu.VMEM((PW, size), BF16),
        pltpu.VMEM((ny, tall, 2 * PW), F32),
        pltpu.VMEM((tall, 2 * PW), F32),
        pltpu.VMEM((nx, tall, 2 * PW), F32),
        pltpu.VMEM((ny, tall, 2 * PW), F32),
        pltpu.VMEM((low, 2 * PW), F32),
        pltpu.VMEM((nz, low, 2 * PW), F32),
        pltpu.VMEM((low, 2 * PW), F32),
        pltpu.VMEM((low, 2 * PW), F32),
        pltpu.VMEM((low, 2 * PW), F32),
        pltpu.VMEM((ny, low, 2 * PW), F32),
        dma((1,)), dma((3, nz)), dma((nz,)), dma((7, ny)), dma((7, ny)),
        dma((3, nx)), dma((3, nx)), dma((nz,)), dma((nz,)),
        dma((5,)), dma((4,)), dma((1,)),
    ]
    vmem = pl.BlockSpec(memory_space=pltpu.VMEM)
    left, right = pl.pallas_call(
        functools.partial(exchange, shape),
        out_shape=(
            pltpu.VMEM((size, 2 * PW), BF16),
            pltpu.VMEM((2 * PW, size), BF16),
        ),
        in_specs=[pl.BlockSpec(memory_space=pl.ANY)],
        out_specs=(vmem, vmem),
        scratch_shapes=scratch,
        compiler_params=pltpu.CompilerParams(collective_id=0, has_side_effects=True),
        name="exchange",
    )(matrix)
    return matrix - dot(left, right, ((1,), (0,)))


def grid_of(mesh):
    rows, cols = mesh.shape["row"], mesh.shape["col"]
    return {(32, 32): (16, 4, 8), (4, 4): (2, 2, 2)}[(rows, cols)]


def solution(mesh):
    return jax.shard_map(
        functools.partial(on_device, grid_of(mesh)),
        mesh=mesh,
        in_specs=(P("row", "col"),),
        out_specs=P("row", "col"),
        check_vma=False,
    )
```

```python
import functools

import jax
import jax.numpy as jnp
from jax import lax
from jax.experimental import pallas as pl
from jax.experimental.pallas import tpu as pltpu
from jax.sharding import PartitionSpec as P

PW = 64
HIGHEST = lax.Precision.HIGHEST
MESH = pl.DeviceIdType.MESH
F32 = jnp.float32
BF16 = jnp.bfloat16


def dot(first, second, dims, precision=None):
    return lax.dot_general(
        first, second, (dims, ((), ())), precision=precision, preferred_element_type=F32
    )


def far_first(count):
    return sorted(range(1, count), key=lambda d: -min(d, count - d))


def two_columns(work, i):
    first = jnp.broadcast_to(work[:, i : i + 1], work.shape)
    second = jnp.broadcast_to(work[:, i + 1 : i + 2], work.shape)
    return first, second


def eliminate(gram):
    rows = lax.broadcasted_iota(jnp.int32, (PW, PW), 0)
    lanes = lax.broadcasted_iota(jnp.int32, (PW, PW), 1)
    tall = lax.broadcasted_iota(jnp.int32, (PW, 2 * PW), 0)
    unit = jnp.where(rows == lanes, 1.0, 0.0).astype(F32)
    work = jnp.concatenate([gram, unit], axis=1)
    for i in range(0, PW, 2):
        first, second = two_columns(work, i)
        a, b = first[i : i + 1], second[i : i + 1]
        e, d = first[i + 1 : i + 2], second[i + 1 : i + 2]
        over_a = 1.0 / a
        over_q = a / (a * d - b * e)
        scaled = first * over_a
        rest = (second - scaled * b) * over_q
        top, low = work[i : i + 1], work[i + 1 : i + 2]
        low = low - (e * over_a) * top
        work = work - jnp.where(tall > i, scaled, 0.0) * top
        work = work - jnp.where(tall > i + 1, rest, 0.0) * low
    upper, lower = work[:, :PW], work[:, PW:]
    diagonal = jnp.sum(jnp.where(rows == lanes, upper, 0.0), axis=1, keepdims=True)
    root = 1.0 / jnp.sqrt(diagonal)
    return jnp.where(lanes >= rows, upper, 0.0) * root, jnp.where(lanes <= rows, lower, 0.0) * root


def invert(coupling):
    rows = lax.broadcasted_iota(jnp.int32, (PW, PW), 0)
    lanes = lax.broadcasted_iota(jnp.int32, (PW, PW), 1)
    tall = lax.broadcasted_iota(jnp.int32, (PW, 2 * PW), 0)
    unit = jnp.where(rows == lanes, 1.0, 0.0).astype(F32)
    work = jnp.concatenate([coupling, unit], axis=1)
    for i in range(0, PW, 2):
        first, second = two_columns(work, i)
        a, b = first[i : i + 1], second[i : i + 1]
        e, d = first[i + 1 : i + 2], second[i + 1 : i + 2]
        over = 1.0 / (a * d - b * e)
        top, low = work[i : i + 1], work[i + 1 : i + 2]
        new_top = (d * over) * top - (b * over) * low
        new_low = (a * over) * low - (e * over) * top
        work = work - first * new_top - second * new_low
        work = jnp.where(tall == i, new_top, jnp.where(tall == i + 1, new_low, work))
    return work[:, PW : 2 * PW]


def basis_of(left, corner_t, first):
    spread = jnp.concatenate([jnp.zeros((PW, PW), F32), corner_t], axis=1)
    wide = lax.broadcasted_iota(jnp.int32, (PW, 2 * PW), 1)
    placed = jnp.where((wide >= PW) & first, spread, left[:, : 2 * PW].astype(F32))
    return jnp.concatenate([placed.astype(BF16), left[:, 2 * PW :]], axis=1)


def exchange(shape, a_hbm, left_out, right_out,
             a, rowp, colp, gpart,
             li, lj, zp, zs, zr, zx, zi, zh, zj, gs, gr, gx, g, kp, ks, kf, kk,
             a_sem, send_z, send_d, send_y, recv_y, send_x, recv_x, send_k, recv_k,
             recv_b, send_c, recv_c):
    nz, nx, ny = shape
    size = a.shape[0]
    row, col = lax.axis_index("row"), lax.axis_index("col")
    z, c = row // 2, row % 2
    x, y = col // ny, col % ny
    partner = (z * 2 + 1 - c, col)

    def at_z(d):
        return (lax.rem(z + d, nz) * 2 + c, col)

    def at_y(d):
        return (row, x * ny + lax.rem(y + d, ny))

    def across_y(d):
        return (z * 2 + 1 - c, x * ny + lax.rem(y + d, ny))

    def at_x(d):
        return (row, lax.rem(x + d, nx) * ny + y)

    def to_y(d):
        return lax.rem(y + d, ny)

    def from_y(d):
        return lax.rem(y + ny - d, ny)

    def copy(src, dst, send, recv, where):
        return pltpu.make_async_remote_copy(
            src_ref=src, dst_ref=dst, send_sem=send, recv_sem=recv,
            device_id=where, device_id_type=MESH,
        )

    def got(ref, sem):
        copy(ref, ref, sem, sem, partner).wait_recv()

    def sent(ref, sem):
        copy(ref, ref, sem, sem, partner).wait_send()

    fetch = pltpu.make_async_copy(a_hbm, a, a_sem.at[0])
    fetch.start()
    barrier = pltpu.get_barrier_semaphore()
    peers = [at_z(d) for d in range(1, nz)] + [at_y(d) for d in range(1, ny)]
    peers += [at_x(d) for d in range(1, nx)] + [partner]
    peers += [across_y(d) for d in range(1, ny)]
    for peer in peers:
        pl.semaphore_signal(barrier, inc=1, device_id=peer, device_id_type=MESH)
    fetch.wait()

    bands = lax.broadcasted_iota(jnp.int32, (2 * PW, size), 0)
    places = lax.broadcasted_iota(jnp.int32, (2 * PW, size), 1)
    hidden = (bands < PW) & (places < PW)

    @pl.when(col == 0)
    def _():
        panel = jnp.where(hidden & (row == 0), 0.0, a[:, : 2 * PW].T)
        rowp[...] = panel.astype(BF16).reshape(rowp.shape)

    @pl.when(row == 0)
    def _():
        panel = jnp.where(hidden & (col == 0), 0.0, a[: 2 * PW, :])
        half = panel.astype(BF16)
        colp[...] = half.reshape(colp.shape)
        lj[...] = half.reshape(colp.shape)
        gram = dot(panel[:PW], panel[:PW], ((1,), (1,)), HIGHEST)
        cross = dot(half[:PW], half[PW:], ((1,), (1,)))
        right = a[PW : 2 * PW, PW : 2 * PW].astype(BF16).astype(F32)
        top = jnp.concatenate([a[PW : 2 * PW, :PW], right], axis=1)
        top = jnp.where(col == 0, top, 0.0)
        whole = jnp.concatenate([jnp.concatenate([gram, cross], axis=1), top], axis=0)
        gpart[...] = whole.reshape(gpart.shape)

    pl.semaphore_wait(barrier, len(peers))

    @pl.when(row == 0)
    def _():
        for d in far_first(nz):
            copy(colp.at[0], lj.at[0], send_z.at[0, d], recv_b.at[0], at_z(d)).start()
        copy(colp.at[0], lj.at[0], send_c.at[0], recv_b.at[0], partner).start()
        for d in far_first(ny):
            copy(gpart.at[to_y(d)], gs.at[d], send_y.at[1, d], recv_y.at[1, d], at_y(d)).start()
        for d in far_first(nz):
            copy(colp.at[1], lj.at[1], send_z.at[2, d], recv_b.at[3], at_z(d)).start()
        copy(colp.at[1], lj.at[1], send_c.at[2], recv_b.at[3], partner).start()

    @pl.when(col == 0)
    def _():
        for d in far_first(ny):
            copy(rowp.at[d], li.at[d], send_y.at[0, d], recv_b.at[2], at_y(d)).start()
        for d in range(1, nx):
            copy(rowp.at[0], li.at[0], send_x.at[0, d], recv_x.at[0, 0], at_x(d)).start()
        li[0] = rowp[0]

    @pl.when(row == 0)
    def _():
        total = gpart[y]
        for d in range(1, ny):
            got(gs.at[d], recv_y.at[1, d])
            total += gs[d]
        gr[...] = total
        for d in range(1, nx):
            copy(gr, gx.at[d], send_x.at[1, d], recv_x.at[1, d], at_x(d)).start()

    @pl.when((x == 0) & (y != 0))
    def _():
        got(li.at[y], recv_b.at[2])
        for d in range(1, nx):
            copy(li.at[y], li.at[y], send_x.at[0, d], recv_x.at[0, 0], at_x(d)).start()

    @pl.when(row == 0)
    def _():
        total = gr[...]
        for d in range(1, nx):
            got(gx.at[d], recv_x.at[1, d])
            total += gx[d]
        g[y] = total
        for d in far_first(ny):
            copy(g.at[y], g.at[y], send_y.at[4, d], recv_y.at[4, d], at_y(d)).start()

    @pl.when(x != 0)
    def _():
        got(li.at[y], recv_x.at[0, 0])

    def hand_out(which):
        @pl.when(which)
        def _():
            for d in far_first(ny):
                copy(li.at[y], li.at[y], send_y.at[2, d], recv_y.at[2, d], at_y(d)).start()

    @pl.when(col == 0)
    def _():
        for d in far_first(ny):
            copy(rowp.at[0], li.at[0], send_y.at[2, d], recv_y.at[2, d], at_y(d)).start()

    hand_out((col != 0) & (y < ny // 2))

    @pl.when((row != 0) & (c == 0))
    def _():
        got(lj.at[0], recv_b.at[0])
        copy(lj.at[0], lj.at[0], send_c.at[0], recv_b.at[0], partner).start()

    @pl.when(c == 1)
    def _():
        got(lj.at[0], recv_b.at[0])

    part = dot(lj[0], a[...].astype(BF16), ((1,), (1,)))
    zp[...] = part.reshape(zp.shape)
    for d in far_first(ny):
        copy(zp.at[to_y(d)], zs.at[d], send_y.at[3, d], recv_y.at[3, d], at_y(d)).start()

    @pl.when(row == 0)
    def _():
        for d in range(1, ny):
            got(g.at[from_y(d)], recv_y.at[4, d])
        for d in far_first(nz):
            copy(g, g, send_z.at[1, d], recv_b.at[1], at_z(d)).start()
        copy(g, g, send_c.at[1], recv_b.at[1], partner).start()

    total = zp[y]
    for d in range(1, ny):
        got(zs.at[d], recv_y.at[3, d])
        total += zs[d]
    zr[...] = total
    for d in range(1, nx):
        copy(zr, zx.at[d], send_x.at[2, d], recv_x.at[2, d], at_x(d)).start()

    hand_out(y >= ny // 2)

    def panel_from(upper_half):
        for d in range(1, ny):
            there = from_y(d)

            @pl.when((there >= ny // 2) == upper_half)
            def _():
                got(li.at[there], recv_y.at[2, d])

    panel_from(False)
    panel_l = li[: ny // 2].reshape(PW, size)

    for d in range(1, nx):
        got(zx.at[d], recv_x.at[2, d])
        total += zx[d]
    zi[y] = total
    gap = lax.rem(row % ny + ny - y, ny)
    beside = (x == row // ny) & (gap != 0)

    @pl.when(beside)
    def _():
        copy(zi.at[y], zi.at[y], send_y.at[5, gap], recv_y.at[5, gap], (row, row)).start()

    for d in far_first(ny):

        @pl.when(jnp.logical_not(beside & (gap == d)))
        def _():
            copy(zi.at[y], zi.at[y], send_y.at[5, d], recv_y.at[5, d], at_y(d)).start()

    mine = dot(total, panel_l.astype(F32), ((1,), (1,)), HIGHEST)
    mine = jnp.concatenate([mine, mine], axis=1)
    kp[...] = mine
    for d in far_first(nz):
        copy(kp, ks.at[d], send_k.at[d], recv_k.at[d], at_z(d)).start()

    @pl.when((row != 0) & (c == 0))
    def _():
        got(lj.at[1], recv_b.at[3])
        copy(lj.at[1], lj.at[1], send_c.at[2], recv_b.at[3], partner).start()

    @pl.when((row != 0) & (c == 0))
    def _():
        got(g, recv_b.at[1])
        copy(g, g, send_c.at[1], recv_b.at[1], partner).start()

    @pl.when(c == 1)
    def _():
        got(g, recv_b.at[1])

    whole = g[...].reshape(2 * PW, 2 * PW)
    gram, top = whole[:PW, :PW], whole[PW:, :PW]
    rows = lax.broadcasted_iota(jnp.int32, (PW, PW), 0)
    lanes = lax.broadcasted_iota(jnp.int32, (PW, PW), 1)
    on_diagonal = jnp.where(rows == lanes, gram, 0.0)
    diagonal = jnp.sum(on_diagonal, axis=0, keepdims=True)
    across = 1.0 / jnp.sqrt(diagonal)
    down = 1.0 / jnp.sqrt(jnp.sum(on_diagonal, axis=1, keepdims=True))
    unit_upper, inverse_t = eliminate(gram * down * across)
    upper = unit_upper * (diagonal * across)
    inverse_t = inverse_t * across

    for d in range(1, ny):
        got(zi.at[from_y(d)], recv_y.at[5, d])
    images = zi[...].reshape(PW, size)

    @pl.when(row == col)
    def _():
        half = dot(inverse_t, images, ((1,), (0,)), HIGHEST).astype(BF16)
        zh[...] = half
        zj[...] = half
        for d in far_first(nz):
            copy(zh, zj, send_d.at[d], recv_b.at[4], at_z(d)).start()
        copy(zh, zj, send_d.at[0], recv_b.at[4], partner).start()

    for d in range(1, nz):
        got(ks.at[d], recv_k.at[d])
        mine += ks[d]
    kf[...] = mine
    for d in far_first(ny):
        copy(kf, kk.at[c, y], send_y.at[6, d], recv_y.at[6, d], at_y(d)).start()
        copy(kf, kk.at[c, y], send_y.at[7, d], recv_y.at[7, d], across_y(d)).start()
    copy(kf, kk.at[c, y], send_c.at[3], recv_c.at[0], partner).start()
    kk[c, y] = mine

    shifted = top + upper
    coupling = dot(shifted * across, unit_upper, ((0,), (0,)), HIGHEST)
    core = invert(coupling) * down * across
    corner = shifted.astype(BF16)
    change = corner.astype(F32) - top.astype(BF16).astype(F32)
    corner_t = corner.astype(F32).T
    inner = dot(whole[:, PW:], change, ((1,), (0,)), HIGHEST)
    side = inner[:PW] + inner[:PW].T + dot(change, inner[PW:], ((0,), (0,)), HIGHEST)
    mixed = dot(jnp.concatenate([upper, change], axis=0), core, ((1,), (0,)), HIGHEST)

    panel_from(True)
    panel_t = li[ny // 2 :].reshape(PW, size)

    @pl.when(c == 1)
    def _():
        got(lj.at[1], recv_b.at[3])

    basis_i = basis_of(panel_l, corner_t, row == 0)
    basis_j = basis_of(lj[0], corner_t, col == 0)
    left_out[:, :PW] = basis_i.T
    right_out[PW:, :] = basis_j
    high = images.astype(BF16)
    low = (images - high.astype(F32)).astype(BF16)
    def weigh(weights, stack):
        tall = weights.T
        first = tall.astype(BF16)
        rest = tall - first.astype(F32)
        second = rest.astype(BF16)
        third = (rest - second.astype(F32)).astype(BF16)
        parts = dot(jnp.concatenate([first, second, third], axis=0), stack, ((1,), (0,)))
        return parts[:PW] + (parts[PW : 2 * PW] + parts[2 * PW :])

    fixed_i = weigh(
        jnp.concatenate([core, core, mixed[PW:]], axis=0),
        jnp.concatenate([high, low, panel_t], axis=0),
    )
    fixed_j = weigh(mixed[PW:], lj[1])

    @pl.when((row != col) & (c == col % 2))
    def _():
        got(zj, recv_b.at[4])
        copy(zj, zj, send_d.at[0], recv_b.at[4], partner).start()

    for d in range(1, ny):
        got(kk.at[c, from_y(d)], recv_y.at[6, d])
        got(kk.at[1 - c, from_y(d)], recv_y.at[7, d])
    got(kk.at[1 - c, y], recv_c.at[0])
    projection = (kk[0] + kk[1]).reshape(PW, 2 * PW)[:, :PW] + side
    middle = dot(core, projection, ((0,), (0,)), HIGHEST)
    middle = -0.5 * dot(middle, core, ((1,), (0,)), HIGHEST)

    left_out[:, PW:] = (fixed_i + weigh(middle, basis_i)).astype(BF16).T
    fixed_j = fixed_j + weigh(middle, basis_j)

    @pl.when(c != col % 2)
    def _():
        got(zj, recv_b.at[4])

    right_out[:PW, :] = (fixed_j + weigh(mixed[:PW], zj[...])).astype(BF16)

    for d in range(1, ny):
        sent(li.at[0], send_y.at[2, d])
        sent(zr, send_y.at[3, d])
        sent(zr, send_y.at[5, d])
        sent(kp, send_y.at[6, d])
        sent(kp, send_y.at[7, d])
    for d in range(1, nx):
        sent(zr, send_x.at[2, d])
    for d in range(1, nz):
        sent(kp, send_k.at[d])
    sent(kp, send_c.at[3])

    @pl.when(x == 0)
    def _():
        for d in range(1, nx):
            sent(li.at[0], send_x.at[0, d])

    @pl.when(col == 0)
    def _():
        for d in range(1, ny):
            sent(li.at[0], send_y.at[0, d])

    @pl.when(row == 0)
    def _():
        for d in range(1, ny):
            sent(gr, send_y.at[1, d])
            sent(gr, send_y.at[4, d])
        for d in range(1, nx):
            sent(gr, send_x.at[1, d])
        for d in range(1, nz):
            sent(lj.at[0], send_z.at[0, d])
            sent(g, send_z.at[1, d])
            sent(lj.at[1], send_z.at[2, d])

    @pl.when(c == 0)
    def _():
        sent(lj.at[0], send_c.at[0])
        sent(g, send_c.at[1])
        sent(lj.at[1], send_c.at[2])

    @pl.when(c == col % 2)
    def _():
        sent(zh, send_d.at[0])

    @pl.when(row == col)
    def _():
        for d in range(1, nz):
            sent(zh, send_d.at[d])


def subtract(a_ref, left_ref, right_ref, out_ref):
    out_ref[...] = a_ref[...] - dot(left_ref[...], right_ref[...], ((1,), (0,)))


def on_device(shape, matrix):
    nz, nx, ny = shape
    size = matrix.shape[0]
    tall, low = 2 * PW // ny, PW // ny
    dma = pltpu.SemaphoreType.DMA
    scratch = [
        pltpu.VMEM((size, size), F32),
        pltpu.VMEM((ny, tall, size), BF16),
        pltpu.VMEM((2, PW, size), BF16),
        pltpu.VMEM((ny, tall, 2 * PW), F32),
        pltpu.VMEM((ny, tall, size), BF16),
        pltpu.VMEM((2, PW, size), BF16),
        pltpu.VMEM((ny, low, size), F32),
        pltpu.VMEM((ny, low, size), F32),
        pltpu.VMEM((low, size), F32),
        pltpu.VMEM((nx, low, size), F32),
        pltpu.VMEM((ny, low, size), F32),
        pltpu.VMEM((PW, size), BF16),
        pltpu.VMEM((PW, size), BF16),
        pltpu.VMEM((ny, tall, 2 * PW), F32),
        pltpu.VMEM((tall, 2 * PW), F32),
        pltpu.VMEM((nx, tall, 2 * PW), F32),
        pltpu.VMEM((ny, tall, 2 * PW), F32),
        pltpu.VMEM((low, 2 * PW), F32),
        pltpu.VMEM((nz, low, 2 * PW), F32),
        pltpu.VMEM((low, 2 * PW), F32),
        pltpu.VMEM((2, ny, low, 2 * PW), F32),
        dma((1,)), dma((3, nz)), dma((nz,)), dma((8, ny)), dma((8, ny)),
        dma((3, nx)), dma((3, nx)), dma((nz,)), dma((nz,)),
        dma((5,)), dma((4,)), dma((1,)),
    ]
    vmem = pl.BlockSpec(memory_space=pltpu.VMEM)
    left, right = pl.pallas_call(
        functools.partial(exchange, shape),
        out_shape=(
            pltpu.VMEM((size, 2 * PW), BF16),
            pltpu.VMEM((2 * PW, size), BF16),
        ),
        in_specs=[pl.BlockSpec(memory_space=pl.ANY)],
        out_specs=(vmem, vmem),
        scratch_shapes=scratch,
        compiler_params=pltpu.CompilerParams(collective_id=0, has_side_effects=True),
        name="exchange",
    )(matrix)
    return matrix - dot(left, right, ((1,), (0,)))


def grid_of(mesh):
    rows, cols = mesh.shape["row"], mesh.shape["col"]
    return {(32, 32): (16, 4, 8), (4, 4): (2, 2, 2)}[(rows, cols)]


def solution(mesh):
    return jax.shard_map(
        functools.partial(on_device, grid_of(mesh)),
        mesh=mesh,
        in_specs=(P("row", "col"),),
        out_specs=P("row", "col"),
        check_vma=False,
    )
```

```python
import functools

import jax
import jax.numpy as jnp
from jax import lax
from jax.experimental import pallas as pl
from jax.experimental.pallas import tpu as pltpu
from jax.sharding import PartitionSpec as P

PW = 64
HIGHEST = lax.Precision.HIGHEST
MESH = pl.DeviceIdType.MESH
F32 = jnp.float32
BF16 = jnp.bfloat16


def dot(first, second, dims, precision=None):
    return lax.dot_general(
        first, second, (dims, ((), ())), precision=precision, preferred_element_type=F32
    )


def far_first(count):
    return sorted(range(1, count), key=lambda d: -min(d, count - d))


def in_parts(value):
    first = value.astype(BF16).astype(F32)
    rest = value - first
    second = rest.astype(BF16).astype(F32)
    return jnp.concatenate([first, second, rest - second], axis=0).astype(BF16)


def two_columns(work, i):
    first = jnp.broadcast_to(work[:, i : i + 1], work.shape)
    second = jnp.broadcast_to(work[:, i + 1 : i + 2], work.shape)
    return first, second


def eliminate(gram):
    rows = lax.broadcasted_iota(jnp.int32, (PW, PW), 0)
    lanes = lax.broadcasted_iota(jnp.int32, (PW, PW), 1)
    tall = lax.broadcasted_iota(jnp.int32, (PW, 2 * PW), 0)
    unit = jnp.where(rows == lanes, 1.0, 0.0).astype(F32)
    work = jnp.concatenate([gram, unit], axis=1)
    for i in range(0, PW, 2):
        first, second = two_columns(work, i)
        a, b = first[i : i + 1], second[i : i + 1]
        e, d = first[i + 1 : i + 2], second[i + 1 : i + 2]
        over_a = 1.0 / a
        over_q = a / (a * d - b * e)
        scaled = first * over_a
        rest = (second - scaled * b) * over_q
        top, low = work[i : i + 1], work[i + 1 : i + 2]
        low = low - (e * over_a) * top
        work = work - jnp.where(tall > i, scaled, 0.0) * top
        work = work - jnp.where(tall > i + 1, rest, 0.0) * low
    upper, lower = work[:, :PW], work[:, PW:]
    diagonal = jnp.sum(jnp.where(rows == lanes, upper, 0.0), axis=1, keepdims=True)
    root = 1.0 / jnp.sqrt(diagonal)
    return jnp.where(lanes >= rows, upper, 0.0) * root, jnp.where(lanes <= rows, lower, 0.0) * root


def invert(coupling):
    rows = lax.broadcasted_iota(jnp.int32, (PW, PW), 0)
    lanes = lax.broadcasted_iota(jnp.int32, (PW, PW), 1)
    tall = lax.broadcasted_iota(jnp.int32, (PW, 2 * PW), 0)
    unit = jnp.where(rows == lanes, 1.0, 0.0).astype(F32)
    work = jnp.concatenate([coupling, unit], axis=1)
    for i in range(0, PW, 2):
        first, second = two_columns(work, i)
        a, b = first[i : i + 1], second[i : i + 1]
        e, d = first[i + 1 : i + 2], second[i + 1 : i + 2]
        over = 1.0 / (a * d - b * e)
        top, low = work[i : i + 1], work[i + 1 : i + 2]
        new_top = (d * over) * top - (b * over) * low
        new_low = (a * over) * low - (e * over) * top
        work = work - first * new_top - second * new_low
        work = jnp.where(tall == i, new_top, jnp.where(tall == i + 1, new_low, work))
    return work[:, PW : 2 * PW]


def basis_of(left, corner_t, first):
    spread = jnp.concatenate([jnp.zeros((PW, PW), F32), corner_t], axis=1)
    wide = lax.broadcasted_iota(jnp.int32, (PW, 2 * PW), 1)
    placed = jnp.where((wide >= PW) & first, spread, left[:, : 2 * PW].astype(F32))
    return jnp.concatenate([placed.astype(BF16), left[:, 2 * PW :]], axis=1)


def exchange(shape, a_hbm, left_out, right_out,
             a, a_half, rowp, colp, gpart,
             li, lj, zp, zs, zr, zx, zi, zh, zj, gs, gr, gx, g, kp, ks, kf, kk,
             a_sem, send_z, send_d, send_y, recv_y, send_x, recv_x, send_k, recv_k,
             recv_b, send_c, recv_c):
    nz, nx, ny = shape
    size = a.shape[0]
    row, col = lax.axis_index("row"), lax.axis_index("col")
    z, c = row // 2, row % 2
    x, y = col // ny, col % ny
    partner = (z * 2 + 1 - c, col)

    def at_z(d):
        return (lax.rem(z + d, nz) * 2 + c, col)

    def at_y(d):
        return (row, x * ny + lax.rem(y + d, ny))

    def across_y(d):
        return (z * 2 + 1 - c, x * ny + lax.rem(y + d, ny))

    def at_x(d):
        return (row, lax.rem(x + d, nx) * ny + y)

    def to_y(d):
        return lax.rem(y + d, ny)

    def from_y(d):
        return lax.rem(y + ny - d, ny)

    def copy(src, dst, send, recv, where):
        return pltpu.make_async_remote_copy(
            src_ref=src, dst_ref=dst, send_sem=send, recv_sem=recv,
            device_id=where, device_id_type=MESH,
        )

    def got(ref, sem):
        copy(ref, ref, sem, sem, partner).wait_recv()

    def sent(ref, sem):
        copy(ref, ref, sem, sem, partner).wait_send()

    fetch = pltpu.make_async_copy(a_hbm, a, a_sem.at[0])
    fetch.start()
    barrier = pltpu.get_barrier_semaphore()
    peers = [at_z(d) for d in range(1, nz)] + [at_y(d) for d in range(1, ny)]
    peers += [at_x(d) for d in range(1, nx)] + [partner]
    peers += [across_y(d) for d in range(1, ny)]
    for peer in peers:
        pl.semaphore_signal(barrier, inc=1, device_id=peer, device_id_type=MESH)
    fetch.wait()
    a_half[...] = a[...].astype(BF16)

    bands = lax.broadcasted_iota(jnp.int32, (2 * PW, size), 0)
    places = lax.broadcasted_iota(jnp.int32, (2 * PW, size), 1)
    hidden = (bands < PW) & (places < PW)

    @pl.when(col == 0)
    def _():
        panel = jnp.where(hidden & (row == 0), 0.0, a[:, : 2 * PW].T)
        rowp[...] = panel.astype(BF16).reshape(rowp.shape)

    @pl.when(row == 0)
    def _():
        panel = jnp.where(hidden & (col == 0), 0.0, a[: 2 * PW, :])
        half = panel.astype(BF16)
        colp[...] = half.reshape(colp.shape)
        lj[...] = half.reshape(colp.shape)
        gram = dot(panel[:PW], panel[:PW], ((1,), (1,)), HIGHEST)
        cross = dot(half[:PW], half[PW:], ((1,), (1,)))
        right = a[PW : 2 * PW, PW : 2 * PW].astype(BF16).astype(F32)
        top = jnp.concatenate([a[PW : 2 * PW, :PW], right], axis=1)
        top = jnp.where(col == 0, top, 0.0)
        whole = jnp.concatenate([jnp.concatenate([gram, cross], axis=1), top], axis=0)
        gpart[...] = whole.reshape(gpart.shape)

    pl.semaphore_wait(barrier, len(peers))

    @pl.when(row == 0)
    def _():
        for d in far_first(nz):
            copy(colp.at[0], lj.at[0], send_z.at[0, d], recv_b.at[0], at_z(d)).start()
        copy(colp.at[0], lj.at[0], send_c.at[0], recv_b.at[0], partner).start()
        for d in far_first(ny):
            copy(gpart.at[to_y(d)], gs.at[d], send_y.at[1, d], recv_y.at[1, d], at_y(d)).start()
        for d in far_first(nz):
            copy(colp.at[1], lj.at[1], send_z.at[2, d], recv_b.at[3], at_z(d)).start()
        copy(colp.at[1], lj.at[1], send_c.at[2], recv_b.at[3], partner).start()

    @pl.when(col == 0)
    def _():
        for d in far_first(ny):
            copy(rowp.at[d], li.at[d], send_y.at[0, d], recv_b.at[2], at_y(d)).start()
        for d in range(1, nx):
            copy(rowp.at[0], li.at[0], send_x.at[0, d], recv_x.at[0, 0], at_x(d)).start()
        li[0] = rowp[0]

    @pl.when(row == 0)
    def _():
        total = gpart[y]
        for d in range(1, ny):
            got(gs.at[d], recv_y.at[1, d])
            total += gs[d]
        gr[...] = total
        for d in range(1, nx):
            copy(gr, gx.at[d], send_x.at[1, d], recv_x.at[1, d], at_x(d)).start()

    @pl.when((x == 0) & (y != 0))
    def _():
        got(li.at[y], recv_b.at[2])
        for d in range(1, nx):
            copy(li.at[y], li.at[y], send_x.at[0, d], recv_x.at[0, 0], at_x(d)).start()

    @pl.when(row == 0)
    def _():
        total = gr[...]
        for d in range(1, nx):
            got(gx.at[d], recv_x.at[1, d])
            total += gx[d]
        g[y] = total
        for d in far_first(ny):
            copy(g.at[y], g.at[y], send_y.at[4, d], recv_y.at[4, d], at_y(d)).start()

    @pl.when(x != 0)
    def _():
        got(li.at[y], recv_x.at[0, 0])

    def hand_out(which):
        @pl.when(which)
        def _():
            for d in far_first(ny):
                copy(li.at[y], li.at[y], send_y.at[2, d], recv_y.at[2, d], at_y(d)).start()

    @pl.when(col == 0)
    def _():
        for d in far_first(ny):
            copy(rowp.at[0], li.at[0], send_y.at[2, d], recv_y.at[2, d], at_y(d)).start()

    hand_out((col != 0) & (y < ny // 2))

    @pl.when((row != 0) & (c == 0))
    def _():
        got(lj.at[0], recv_b.at[0])
        copy(lj.at[0], lj.at[0], send_c.at[0], recv_b.at[0], partner).start()

    @pl.when(c == 1)
    def _():
        got(lj.at[0], recv_b.at[0])

    part = dot(lj[0], a_half[...], ((1,), (1,)))
    zp[...] = part.reshape(zp.shape)
    for d in far_first(ny):
        copy(zp.at[to_y(d)], zs.at[d], send_y.at[3, d], recv_y.at[3, d], at_y(d)).start()

    @pl.when(row == 0)
    def _():
        for d in range(1, ny):
            got(g.at[from_y(d)], recv_y.at[4, d])
        for d in far_first(nz):
            copy(g, g, send_z.at[1, d], recv_b.at[1], at_z(d)).start()
        copy(g, g, send_c.at[1], recv_b.at[1], partner).start()

    total = zp[y]
    for d in range(1, ny):
        got(zs.at[d], recv_y.at[3, d])
        total += zs[d]
    zr[...] = total
    for d in range(1, nx):
        copy(zr, zx.at[d], send_x.at[2, d], recv_x.at[2, d], at_x(d)).start()

    hand_out(y >= ny // 2)

    def panel_from(upper_half):
        for d in range(1, ny):
            there = from_y(d)

            @pl.when((there >= ny // 2) == upper_half)
            def _():
                got(li.at[there], recv_y.at[2, d])

    panel_from(False)
    panel_l = li[: ny // 2].reshape(PW, size)

    for d in range(1, nx):
        got(zx.at[d], recv_x.at[2, d])
        total += zx[d]
    zi[y] = total
    gap = lax.rem(row % ny + ny - y, ny)
    beside = (x == row // ny) & (gap != 0)

    @pl.when(beside)
    def _():
        copy(zi.at[y], zi.at[y], send_y.at[5, gap], recv_y.at[5, gap], (row, row)).start()

    for d in far_first(ny):

        @pl.when(jnp.logical_not(beside & (gap == d)))
        def _():
            copy(zi.at[y], zi.at[y], send_y.at[5, d], recv_y.at[5, d], at_y(d)).start()

    mine = dot(in_parts(total), panel_l, ((1,), (1,)))
    low = total.shape[0]
    mine = mine[:low] + (mine[low : 2 * low] + mine[2 * low :])
    mine = jnp.concatenate([mine[: low // 2], mine[low // 2 :]], axis=1)
    kp[...] = mine
    for d in far_first(nz):
        copy(kp, ks.at[d], send_k.at[d], recv_k.at[d], at_z(d)).start()

    @pl.when((row != 0) & (c == 0))
    def _():
        got(lj.at[1], recv_b.at[3])
        copy(lj.at[1], lj.at[1], send_c.at[2], recv_b.at[3], partner).start()

    @pl.when((row != 0) & (c == 0))
    def _():
        got(g, recv_b.at[1])
        copy(g, g, send_c.at[1], recv_b.at[1], partner).start()

    @pl.when(c == 1)
    def _():
        got(g, recv_b.at[1])

    whole = g[...].reshape(2 * PW, 2 * PW)
    gram, top = whole[:PW, :PW], whole[PW:, :PW]
    rows = lax.broadcasted_iota(jnp.int32, (PW, PW), 0)
    lanes = lax.broadcasted_iota(jnp.int32, (PW, PW), 1)
    on_diagonal = jnp.where(rows == lanes, gram, 0.0)
    diagonal = jnp.sum(on_diagonal, axis=0, keepdims=True)
    across = 1.0 / jnp.sqrt(diagonal)
    down = 1.0 / jnp.sqrt(jnp.sum(on_diagonal, axis=1, keepdims=True))
    unit_upper, inverse_t = eliminate(gram * down * across)
    upper = unit_upper * (diagonal * across)
    inverse_t = inverse_t * across

    for d in range(1, ny):
        got(zi.at[from_y(d)], recv_y.at[5, d])
    images = zi[...].reshape(PW, size)

    @pl.when(row == col)
    def _():
        half = dot(inverse_t, images, ((1,), (0,)), HIGHEST).astype(BF16)
        zh[...] = half
        zj[...] = half
        for d in far_first(nz):
            copy(zh, zj, send_d.at[d], recv_b.at[4], at_z(d)).start()
        copy(zh, zj, send_d.at[0], recv_b.at[4], partner).start()

    for d in range(1, nz):
        got(ks.at[d], recv_k.at[d])
        mine += ks[d]
    kf[...] = mine
    for d in far_first(ny):
        copy(kf, kk.at[c, y], send_y.at[6, d], recv_y.at[6, d], at_y(d)).start()
        copy(kf, kk.at[c, y], send_y.at[7, d], recv_y.at[7, d], across_y(d)).start()
    copy(kf, kk.at[c, y], send_c.at[3], recv_c.at[0], partner).start()
    kk[c, y] = mine

    shifted = top + upper
    coupling = dot(shifted * across, unit_upper, ((0,), (0,)), HIGHEST)
    core = invert(coupling) * down * across
    corner = shifted.astype(BF16)
    change = corner.astype(F32) - top.astype(BF16).astype(F32)
    corner_t = corner.astype(F32).T
    inner = dot(whole[:, PW:], change, ((1,), (0,)), HIGHEST)
    side = inner[:PW] + inner[:PW].T + dot(change, inner[PW:], ((0,), (0,)), HIGHEST)
    mixed = dot(jnp.concatenate([upper, change], axis=0), core, ((1,), (0,)), HIGHEST)

    panel_from(True)
    panel_t = li[ny // 2 :].reshape(PW, size)

    @pl.when(c == 1)
    def _():
        got(lj.at[1], recv_b.at[3])

    basis_i = basis_of(panel_l, corner_t, row == 0)
    basis_j = basis_of(lj[0], corner_t, col == 0)
    left_out[:, :PW] = basis_i.T
    right_out[PW:, :] = basis_j
    high = images.astype(BF16)
    below = (images - high.astype(F32)).astype(BF16)
    def weigh(weights, stack):
        parts = dot(in_parts(weights.T), stack, ((1,), (0,)))
        return parts[:PW] + (parts[PW : 2 * PW] + parts[2 * PW :])

    fixed_i = weigh(
        jnp.concatenate([core, core, mixed[PW:]], axis=0),
        jnp.concatenate([high, below, panel_t], axis=0),
    )
    fixed_j = weigh(mixed[PW:], lj[1])

    @pl.when((row != col) & (c == col % 2))
    def _():
        got(zj, recv_b.at[4])
        copy(zj, zj, send_d.at[0], recv_b.at[4], partner).start()

    for d in range(1, ny):
        got(kk.at[c, from_y(d)], recv_y.at[6, d])
        got(kk.at[1 - c, from_y(d)], recv_y.at[7, d])
    got(kk.at[1 - c, y], recv_c.at[0])
    halves = kk[0] + kk[1]
    halves = jnp.concatenate([halves[:, :, :PW], halves[:, :, PW:]], axis=1)
    projection = halves.reshape(PW, PW) + side
    middle = dot(core, projection, ((0,), (0,)), HIGHEST)
    middle = -0.5 * dot(middle, core, ((1,), (0,)), HIGHEST)

    left_out[:, PW:] = (fixed_i + weigh(middle, basis_i)).astype(BF16).T
    fixed_j = fixed_j + weigh(middle, basis_j)

    @pl.when(c != col % 2)
    def _():
        got(zj, recv_b.at[4])

    right_out[:PW, :] = (fixed_j + weigh(mixed[:PW], zj[...])).astype(BF16)

    for d in range(1, ny):
        sent(li.at[0], send_y.at[2, d])
        sent(zr, send_y.at[3, d])
        sent(zr, send_y.at[5, d])
        sent(kp, send_y.at[6, d])
        sent(kp, send_y.at[7, d])
    for d in range(1, nx):
        sent(zr, send_x.at[2, d])
    for d in range(1, nz):
        sent(kp, send_k.at[d])
    sent(kp, send_c.at[3])

    @pl.when(x == 0)
    def _():
        for d in range(1, nx):
            sent(li.at[0], send_x.at[0, d])

    @pl.when(col == 0)
    def _():
        for d in range(1, ny):
            sent(li.at[0], send_y.at[0, d])

    @pl.when(row == 0)
    def _():
        for d in range(1, ny):
            sent(gr, send_y.at[1, d])
            sent(gr, send_y.at[4, d])
        for d in range(1, nx):
            sent(gr, send_x.at[1, d])
        for d in range(1, nz):
            sent(lj.at[0], send_z.at[0, d])
            sent(g, send_z.at[1, d])
            sent(lj.at[1], send_z.at[2, d])

    @pl.when(c == 0)
    def _():
        sent(lj.at[0], send_c.at[0])
        sent(g, send_c.at[1])
        sent(lj.at[1], send_c.at[2])

    @pl.when(c == col % 2)
    def _():
        sent(zh, send_d.at[0])

    @pl.when(row == col)
    def _():
        for d in range(1, nz):
            sent(zh, send_d.at[d])


def subtract(a_ref, left_ref, right_ref, out_ref):
    out_ref[...] = a_ref[...] - dot(left_ref[...], right_ref[...], ((1,), (0,)))


def on_device(shape, matrix):
    nz, nx, ny = shape
    size = matrix.shape[0]
    tall, low = 2 * PW // ny, PW // ny
    dma = pltpu.SemaphoreType.DMA
    scratch = [
        pltpu.VMEM((size, size), F32),
        pltpu.VMEM((size, size), BF16),
        pltpu.VMEM((ny, tall, size), BF16),
        pltpu.VMEM((2, PW, size), BF16),
        pltpu.VMEM((ny, tall, 2 * PW), F32),
        pltpu.VMEM((ny, tall, size), BF16),
        pltpu.VMEM((2, PW, size), BF16),
        pltpu.VMEM((ny, low, size), F32),
        pltpu.VMEM((ny, low, size), F32),
        pltpu.VMEM((low, size), F32),
        pltpu.VMEM((nx, low, size), F32),
        pltpu.VMEM((ny, low, size), F32),
        pltpu.VMEM((PW, size), BF16),
        pltpu.VMEM((PW, size), BF16),
        pltpu.VMEM((ny, tall, 2 * PW), F32),
        pltpu.VMEM((tall, 2 * PW), F32),
        pltpu.VMEM((nx, tall, 2 * PW), F32),
        pltpu.VMEM((ny, tall, 2 * PW), F32),
        pltpu.VMEM((low // 2, 2 * PW), F32),
        pltpu.VMEM((nz, low // 2, 2 * PW), F32),
        pltpu.VMEM((low // 2, 2 * PW), F32),
        pltpu.VMEM((2, ny, low // 2, 2 * PW), F32),
        dma((1,)), dma((3, nz)), dma((nz,)), dma((8, ny)), dma((8, ny)),
        dma((3, nx)), dma((3, nx)), dma((nz,)), dma((nz,)),
        dma((5,)), dma((4,)), dma((1,)),
    ]
    vmem = pl.BlockSpec(memory_space=pltpu.VMEM)
    left, right = pl.pallas_call(
        functools.partial(exchange, shape),
        out_shape=(
            pltpu.VMEM((size, 2 * PW), BF16),
            pltpu.VMEM((2 * PW, size), BF16),
        ),
        in_specs=[pl.BlockSpec(memory_space=pl.ANY)],
        out_specs=(vmem, vmem),
        scratch_shapes=scratch,
        compiler_params=pltpu.CompilerParams(collective_id=0, has_side_effects=True),
        name="exchange",
    )(matrix)
    return matrix - dot(left, right, ((1,), (0,)))


def grid_of(mesh):
    rows, cols = mesh.shape["row"], mesh.shape["col"]
    return {(32, 32): (16, 4, 8), (4, 4): (2, 2, 2)}[(rows, cols)]


def solution(mesh):
    return jax.shard_map(
        functools.partial(on_device, grid_of(mesh)),
        mesh=mesh,
        in_specs=(P("row", "col"),),
        out_specs=P("row", "col"),
        check_vma=False,
    )
```
